768 devices in a mesh: grp: 32 (over x, y), tp: 8 (over z_hi, core), pp: 3 (over z_lo).
Axes of the slice: x: 4, y: 8, z: 12 (z_hi: 4, z_lo: 3; z = z_hi * 3 + z_lo), core: 2. Of those that a mesh axis runs over, the one named last changes fastest.
Arguments:
- vision: bfloat16 [3, 2048, 3200], P('pp', 'grp'), may hold values from -6 to 6
- text_embed: bfloat16 [3, 8192, 8192], P('pp', 'grp', 'tp'), may hold values from -6 to 6
- target: int32 [3, 2048, 1], P('pp', 'grp'), may hold values from 0 to 31; in each aligned block of 64 rows (0 to 63, 64 to 127, ..., all dimensions but the last counted through in order) at most 4 rows name the same one
- slot_place: int32 [3, 32, 128], P('pp', 'grp'), may hold values from 0 to 255, as said below
- loss_mask: int32 [3, 8192], P('pp', 'grp'), may hold values from 0 to 1
- w_proj: bfloat16 [3200, 8192], P(None, 'tp'), may hold values from -0.109375 to 0.109375
- w_value: bfloat16 [8192, 1024], P('tp'), may hold values from -0.0625 to 0.0625
- cotangent: bfloat16 [3, 8192, 1024], P('pp', 'grp'), may hold values from -6 to 6
Outputs:
- values: bfloat16 [3, 8192, 1024], P('pp', ('grp', 'tp'))
- vision_grad: bfloat16 [3, 2048, 3200], P('pp', ('grp', 'tp'))
The draws below stay inside these ranges and needn't reach their ends.
Inputs may be any that keep to these rules, and one draw needn't show every extreme that they name: `target`: within each aligned block of 64 rows of one section no rank is named more than 4 times. `slot_place`: for each section and rank, 128 distinct positions.
All inputs are finite; a program needn't handle non-finite values.
Results may differ from the reference program's by a relative error of at most 0.0049.
Values may be sent and summed in bfloat16 or wider, within the bound.
A program may use at most 32 MiB of HBM per device.

```python
import math
import jax
import jax.numpy as jnp
import numpy as np

D_VIS = 3200
D = 8192
KVD = 1024
IMG_DEV = 64
SEQ = 256
RANKS = 32
SECTIONS = 3
CAP = 4
SLOTS = 128
IMG_ROWS = 2048
POS_ROWS = 8192
N_GRP = 32


def draw_slot_place(key, part):
    keys = jax.random.split(jax.random.fold_in(key, 7331), SECTIONS * RANKS)

    def one_rank(rank_key):
        return jax.random.permutation(rank_key, SEQ)[:SLOTS]
    table = jax.vmap(one_rank)(keys)
    return table.reshape(SECTIONS, RANKS, SLOTS).astype(jnp.int32)


def draw_loss_mask(key, part):
    level_key = jax.random.fold_in(key, 4410)
    cell_key = jax.random.fold_in(key, 4412)
    level = jax.random.randint(level_key, (1, 1, 1), 2, 7, dtype=jnp.int32)
    rank_ids = jnp.arange(RANKS, dtype=jnp.int32).reshape(1, RANKS, 1)
    spread = max(RANKS - 1, 1)
    rates = level * (spread + 2 * rank_ids)
    denom = 20 * spread
    draws = jax.random.randint(cell_key, (SECTIONS, RANKS, SEQ), 0, denom, dtype=jnp.int32)
    marked = (draws < rates).astype(jnp.int32)
    return marked.reshape(SECTIONS, RANKS * SEQ).astype(jnp.int32)


def block_levels(stream_key, shape, cuts, least, high):
    factor_of = 1.0
    for dim, blocks in cuts:
        steps = jax.random.uniform(jax.random.fold_in(jax.random.fold_in(stream_key, 6), dim), (blocks,), jnp.float32, least / len(cuts), high / len(cuts))
        factor_of = factor_of * jnp.repeat(jnp.exp(steps), shape[dim] // blocks).reshape((-1,) + (1,) * (len(shape) - 1 - dim))
    return factor_of


def assign_block(stream_key, own, number, rows, count, top, limit, slope):
    sequence = jax.random.permutation(stream_key, count)
    packed, usual = portions_of(count, rows * top, limit, slope, True), portions_of(count, rows * top, limit, slope, False)
    places = jnp.arange(count)

    def named(tallies, rotation):
        used = int((tallies > 0).sum())
        fixed = max(1, used // 4)
        shifted = fixed + (places - fixed + rotation * (used - fixed)) % max(1, count - fixed)
        return jnp.zeros((count,), jnp.int32).at[sequence[jnp.where(places < fixed, places, shifted)]].set(jnp.asarray(tallies, jnp.int32))

    tallies = jnp.where(number % 4 == 0, named(packed, number // 4), named(usual, number - number // 4 - 1))
    mixed = jax.random.permutation(jax.random.fold_in(own, 3), count)
    giver, sink = mixed[0:count // 2 * 2:2], mixed[1:count // 2 * 2:2]
    slack = jnp.minimum(tallies[giver] - 1, limit - tallies[sink]) // 2
    slack = jnp.where((giver == sequence[0]) | (sink == sequence[0]) | (tallies[sink] == 0), 0, jnp.maximum(slack, 0))
    shifted = jax.random.randint(jax.random.fold_in(own, 4), (count // 2,), 0, 1 << 20) % (slack + 1)
    tallies = tallies.at[giver].add(-shifted).at[sink].add(shifted)
    items = jnp.searchsorted(jnp.cumsum(tallies), jnp.arange(rows * top), side="right").astype(jnp.int32)
    listing = items.reshape(top, rows).T
    listing = listing[jax.random.permutation(jax.random.fold_in(own, 1), rows)]
    rotation = jax.random.randint(jax.random.fold_in(own, 2), (rows, 1), 0, top)
    return jnp.take_along_axis(listing, (jnp.arange(top)[None, :] + rotation) % top, axis=1)


def portions_of(amount, total, reach, skew, full):
    weights = [(1 << 20) // math.isqrt(standing ** skew) + 1 for standing in range(1, amount + 1)]
    largest = reach if full else min(reach, max(-(-total // amount), total * weights[0] // sum(weights)))
    least = 1 if total - largest >= amount - 1 else 0
    given, rest = [largest] + [least] * (amount - 1), total - largest - least * (amount - 1)
    while rest > 0:
        free = [i for i in range(1, amount) if given[i] < largest] or [i for i in range(1, amount) if given[i] < reach]
        mass, remaining = sum([weights[i] for i in free]), rest
        for i in free:
            addition = min(reach - given[i], max(1, remaining * weights[i] // mass), rest)
            given[i] = given[i] + addition
            rest = rest - addition
    return np.array(given)


def gaussian(own_key, shape, deviation, most, pieces=(), held_as=jnp.bfloat16):
    entries = deviation * jax.random.normal(own_key, shape, jnp.float32)
    if pieces:
        entries = entries * block_levels(own_key, shape, pieces, -0.22, 0.18)
    return jnp.clip(entries, -most, most).astype(held_as)


def setup_inputs(seed: int = 0) -> dict:
    key_list = jax.random.split(jax.random.key(seed), 9)
    vision = gaussian(key_list[0], (SECTIONS, IMG_ROWS, D_VIS), 1.0, 6.0, ((0, 3), (1, 32)))
    text_embed = gaussian(key_list[1], (SECTIONS, POS_ROWS, D), 1.0, 6.0, ((0, 3), (1, 32), (2, 8)))
    target_keys = jax.random.split(jax.random.fold_in(key_list[2], 1), SECTIONS * IMG_ROWS // IMG_DEV)
    target_turns = jax.random.permutation(jax.random.fold_in(key_list[2], 3), SECTIONS * IMG_ROWS // IMG_DEV)
    target = jax.vmap(lambda own, number: assign_block(jax.random.fold_in(key_list[2], 2), own, number, IMG_DEV, N_GRP, 1, CAP, 2))(target_keys, target_turns).reshape((SECTIONS, IMG_ROWS, 1))
    slot_place = draw_slot_place(jax.random.fold_in(key_list[8], 71), 0)
    loss_mask = draw_loss_mask(jax.random.fold_in(key_list[8], 71), 0)
    w_proj = gaussian(key_list[5], (D_VIS, D), D_VIS ** -0.5, 0.109375, ((1, 8),))
    w_value = gaussian(key_list[6], (D, KVD), D ** -0.5, 0.0625, ((0, 8),))
    cotangent = gaussian(key_list[7], (SECTIONS, POS_ROWS, KVD), 1.0, 6.0, ((0, 3), (1, 32)))
    return dict(vision=vision, text_embed=text_embed, target=target, slot_place=slot_place, loss_mask=loss_mask, w_proj=w_proj, w_value=w_value, cotangent=cotangent)


def reference(vision, text_embed, target, slot_place, loss_mask, w_proj, w_value, cotangent):
    value_list = []
    grad_list = []
    text_total = jnp.float32(0.0)
    for section_idx in range(SECTIONS):
        embedded = jnp.dot(vision[section_idx], w_proj, preferred_element_type=jnp.float32).astype(jnp.bfloat16)
        target_rank = target[section_idx, :, 0].astype(jnp.int32)
        onehot = (target_rank[:, None] == jnp.arange(RANKS, dtype=jnp.int32)[None, :]).astype(jnp.int32)
        blocks = onehot.reshape(RANKS, IMG_DEV, RANKS)
        before = (jnp.cumsum(blocks, axis=1) - blocks).reshape(RANKS * IMG_DEV, RANKS)
        rank_within = jnp.sum(before * onehot, axis=1).astype(jnp.int32)
        source = (jnp.arange(RANKS * IMG_DEV, dtype=jnp.int32) // IMG_DEV).astype(jnp.int32)
        slot_index = (source * CAP + rank_within).astype(jnp.int32)
        position = slot_place[section_idx][target_rank, slot_index].astype(jnp.int32)
        flat_rows = (target_rank * SEQ + position).astype(jnp.int32)
        merged = text_embed[section_idx].at[flat_rows].set(embedded)
        is_image = jnp.zeros((RANKS * SEQ,), jnp.float32).at[flat_rows].set(1.0)
        text_total = text_total + jnp.sum(loss_mask[section_idx].astype(jnp.float32) * (1.0 - is_image))
        value_list.append(jnp.dot(merged, w_value, preferred_element_type=jnp.float32).astype(jnp.bfloat16))
        d_image = jnp.dot(cotangent[section_idx][flat_rows], w_value.T, preferred_element_type=jnp.float32).astype(jnp.bfloat16)
        grad_list.append(jnp.dot(d_image, w_proj.T, preferred_element_type=jnp.float32))
    loss_scale = jnp.float32(SECTIONS * RANKS * SEQ) / text_total
    return jnp.stack(value_list), (jnp.stack(grad_list) * loss_scale).astype(jnp.bfloat16)
```

```python
import functools

import jax
import jax.numpy as jnp
from jax import lax
from jax.experimental import pallas as pl
from jax.experimental.pallas import tpu as pltpu
from jax.sharding import PartitionSpec as P

MESH = pl.DeviceIdType.MESH
BF, F32, I32 = jnp.bfloat16, jnp.float32, jnp.int32


def iota(shape, dim):
    return lax.broadcasted_iota(I32, shape, dim)


def mm(a, b):
    return jnp.dot(a, b, preferred_element_type=F32)


def mm_nt(a, b):
    return lax.dot_general(a, b, (((1,), (1,)), ((), ())), preferred_element_type=F32)


def flag(cond):
    return jnp.where(cond, 1.0, 0.0).astype(F32)


def to_col(row):
    n = row.shape[1]
    return jnp.sum(jnp.where(iota((n, n), 0) == iota((n, n), 1), row, 0), axis=1, keepdims=True)


class Reduce:
    def __init__(self, env, half, pf, pb, pr, sb, r1, fdn, fup, send, recv):
        self.env, self.half = env, half
        self.pf, self.pb, self.pr, self.sb = pf, pb, pr, sb
        core, hi = env["core"], env["hi"]
        h_up, h_dn, h_op = env["h_up"], env["h_dn"], env["h_op"]
        own = lambda h, s: half(sb.at[h], s)
        self.pair = pltpu.make_async_remote_copy(
            pb, pr, send.at[6], recv.at[6], device_id={"tp": env["partner"]}, device_id_type=MESH
        )
        table = [
            (own(h_op, 0), half(r1, 0), "up"),
            (own(h_op, 1), half(r1, 1), "dn"),
            (own(h_up, 1), half(fdn, 1), "up"),
            (own(h_dn, 0), half(fup, 0), "dn"),
            (own(h_up, 0), half(fdn, 0), "up"),
            (own(h_dn, 1), half(fup, 1), "dn"),
        ]
        self.copies = [
            pltpu.make_async_remote_copy(
                src, dst, send.at[i], recv.at[i], device_id={"tp": env[way]}, device_id_type=MESH
            )
            for i, (src, dst, way) in enumerate(table)
        ]
        self.r1, self.fdn, self.fup = r1, fdn, fup

    def start_pair(self):
        self.pb[...] = self.pf[1 - self.env["core"]].astype(BF)
        self.pair.start()

    def begin(self):
        env, half = self.env, self.half
        mine = self.pf.at[env["core"]]
        self.pair.wait_recv()
        for h, s, i in (("h_op", 0, 0), ("h_op", 1, 1), ("h_up", 1, 2), ("h_dn", 0, 3)):
            v = half(mine.at[env[h]], s)[...] + half(self.pr.at[env[h]], s)[...].astype(F32)
            half(self.sb.at[env[h]], s)[...] = v.astype(BF)
            self.copies[i].start()

    def middle(self):
        env, half = self.env, self.half
        mine = self.pf.at[env["core"]]
        for h, s, i in (("h_up", 0, 0), ("h_dn", 1, 1)):
            v = half(mine.at[env[h]], s)[...] + half(self.pr.at[env[h]], s)[...].astype(F32)
            self.copies[i].wait_recv()
            v = v + half(self.r1, s)[...].astype(F32)
            half(self.sb.at[env[h]], s)[...] = v.astype(BF)
            self.copies[4 + i].start()

    def end(self):
        env = self.env
        for i in (2, 3, 4, 5):
            self.copies[i].wait_recv()
        return (
            self.pf[env["core"], env["hi"]]
            + self.pr[env["hi"]].astype(F32)
            + self.fdn[...].astype(F32)
            + self.fup[...].astype(F32)
        )

    def drain(self):
        self.pair.wait_send()
        for c in self.copies:
            c.wait_send()


def kernel(
    sizes, target, place, loss, vision, w_proj, w_value, text, cot, values_out, grad_out,
    target_v, place_v, loss_v, vision_v, wp_v, wv_v, text_v, cot_v,
    emb_acc, tpf, tpb, tpr, tsb, tr1, tfd, tfu,
    ipf, ipb, ipr, isb, ir1, ifd, ifu,
    gpf, gpb, gpr, gsb, gr1, gfd, gfu,
    xcot, rcot, xmeta, rmeta, ximg, rimg, chalf, zs, zr, tot_s, tot_r,
    load_sem, t_send, t_recv, i_send, i_recv, g_send, g_recv, a_send, a_recv, z_send, z_recv, s_sem, p_send, p_recv,
):
    groups, tps, pps, parts = sizes
    grp, tp, pp = lax.axis_index("grp"), lax.axis_index("tp"), lax.axis_index("pp")
    core, hi = lax.rem(tp, 2), tp // 2
    chips = tps // 2
    env = dict(
        core=core, hi=hi, partner=tp + 1 - 2 * core,
        up=lax.rem(tp + 2, tps), dn=lax.rem(tp + tps - 2, tps),
        h_up=lax.rem(hi + 1, chips), h_dn=lax.rem(hi + chips - 1, chips), h_op=lax.rem(hi + 2, chips),
    )
    img, width = vision_v.shape[0], wp_v.shape[1]
    dvis, seq, kvd = wp_v.shape[0], text_v.shape[0], wv_v.shape[1]
    half_kv = kvd // 2
    slots = place_v.shape[1]
    cap = slots // groups
    kchunk = dvis // parts

    pairs = [
        (target, target_v), (place, place_v), (loss, loss_v), (w_value, wv_v), (text.at[0], text_v),
        (cot.at[0, :, pl.ds(pl.multiple_of(core * half_kv, 128), half_kv)], cot_v), (vision.at[0], vision_v),
    ] + [(w_proj.at[pl.ds(i * kchunk, kchunk)], wp_v.at[pl.ds(i * kchunk, kchunk)]) for i in range(parts)]
    loads = [pltpu.make_async_copy(s, d, load_sem.at[i]) for i, (s, d) in enumerate(pairs)]
    for c in loads:
        c.start()
    barrier = pltpu.get_barrier_semaphore()

    def greet(axis, me, n):
        @pl.loop(1, n)
        def _(i):
            pl.semaphore_signal(barrier, inc=1, device_id={axis: lax.rem(me + i, n)}, device_id_type=MESH)

    greet("tp", tp, tps)
    greet("grp", grp, groups)
    greet("pp", pp, pps)

    for c in loads[:3]:
        c.wait()
    t_row = target_v[...]
    t_col = to_col(t_row)
    same = t_col == t_row
    k_col = jnp.sum(jnp.where(same & (iota((img, img), 1) < iota((img, img), 0)), 1, 0), axis=1, keepdims=True)
    k_row = jnp.sum(jnp.where(same & (iota((img, img), 0) < iota((img, img), 1)), 1, 0), axis=0, keepdims=True)
    counts = jnp.sum(flag(t_col == iota((img, 128), 1)), axis=0, keepdims=True)
    sp_row = place_v[...]
    sp_col = to_col(sp_row)
    loss_f = loss_v[...].astype(F32)
    at_slot = flag(sp_col == iota((slots, seq), 1))
    mask_slot = jnp.sum(at_slot * loss_f, axis=1, keepdims=True)
    eye = iota((slots, slots), 0) == iota((slots, slots), 1)
    mask_row = jnp.sum(jnp.where(eye, mask_slot, 0.0), axis=0, keepdims=True)
    mask_sum = jnp.sum(loss_f, axis=1, keepdims=True)
    r8 = iota((8, 128), 0)
    meta = jnp.where(r8 == 0, counts, jnp.where(r8 == 1, mask_row, jnp.where(r8 == 2, mask_sum, 0.0)))
    xmeta[...] = meta

    loads[5].wait()
    y = mm(at_slot.astype(BF), cot_v[...]).astype(BF)
    ystack = jnp.concatenate([y[:, 128 * j : 128 * (j + 1)] for j in range(4)], axis=0)
    d_i, d_l = iota((4 * slots, 4 * slots), 0), iota((4 * slots, 4 * slots), 1)
    shuffle = flag(d_l == slots * ((d_i // 4) % 4) + 4 * (d_i // 16) + d_i % 4).astype(BF)
    xcot[...] = mm(shuffle, ystack).astype(BF).reshape(groups, 16, 128)

    loads[3].wait()
    loads[4].wait()
    rows_out = seq // tps
    hr = rows_out // 2
    for n in range(4):
        cols = pl.ds(n * 256, 256)
        res = mm(text_v[...], wv_v[:, cols])
        for t in range(tps):
            for s in range(2):
                r0 = t * rows_out + s * hr
                tpf[t % 2, t // 2, s, :, cols] = res[r0 : r0 + hr]

    loads[6].wait()
    for i in range(parts):
        loads[7 + i].wait()
        part = mm(vision_v[:, i * kchunk : (i + 1) * kchunk], wp_v[i * kchunk : (i + 1) * kchunk, :])
        if i == 0:
            emb_acc[...] = part
        else:
            emb_acc[...] += part
    emb = emb_acc[...].astype(BF)
    for t in range(tps):
        if t % 2 == 0:
            res = mm(emb, wv_v[:, 128 * t : 128 * t + 256])
        piece = res[:, 128 * (t % 2) : 128 * (t % 2) + 128]
        for s in range(2):
            ipf[t % 2, t // 2, s] = piece[s * (img // 2) : (s + 1) * (img // 2)]

    by_lead = lambda ref, s: ref.at[s]
    cut = gsb.shape[-1] // 256 * 128 + 128 * (gsb.shape[-1] // 128 % 2)
    by_lane = lambda ref, s: ref.at[:, pl.ds(0, cut)] if s == 0 else ref.at[:, pl.ds(cut, ref.shape[1] - cut)]
    red_i = Reduce(env, by_lead, ipf, ipb, ipr, isb, ir1, ifd, ifu, i_send, i_recv)
    red_t = Reduce(env, by_lead, tpf, tpb, tpr, tsb, tr1, tfd, tfu, t_send, t_recv)
    red_g = Reduce(env, by_lane, gpf, gpb, gpr, gsb, gr1, gfd, gfu, g_send, g_recv)

    pl.semaphore_wait(barrier, (tps - 1) + (groups - 1) + (pps - 1))

    red_i.start_pair()

    def spread(src, dst, k, whole):
        @pl.loop(1, groups)
        def _(i):
            peer = lax.rem(grp + i, groups)
            pltpu.make_async_remote_copy(
                src if whole else src.at[peer], dst.at[grp], a_send.at[k], a_recv.at[k],
                device_id={"grp": peer}, device_id_type=MESH,
            ).start()

    def collected(ref, sem, n):
        pltpu.make_async_copy(ref.at[pl.ds(0, n)], ref.at[pl.ds(0, n)], sem).wait()

    spread(xcot, rcot, 0, False)
    red_t.start_pair()
    red_i.begin()
    spread(xmeta, rmeta, 1, True)
    red_t.begin()
    red_i.middle()

    collected(rcot, a_recv.at[0], groups - 1)
    rcot[pl.ds(grp, 1)] = xcot[pl.ds(grp, 1)]
    lane = iota((img, 4 * slots), 1)
    pick = jnp.concatenate(
        [flag(lane == 16 * t_col + 4 * j + k_col).astype(BF) for j in range(4)], axis=0
    )
    got = mm(pick, rcot[...].reshape(4 * slots, 128)).astype(BF)
    mine = jnp.concatenate([got[img * j : img * (j + 1)] for j in range(4)], axis=1)
    chalf[pl.ds(core, 1)] = mine[None]
    swap = pltpu.make_async_remote_copy(
        chalf.at[core], chalf.at[core], s_sem.at[0], s_sem.at[1], device_id={"tp": env["partner"]}, device_id_type=MESH
    )
    swap.start()

    vals = red_i.end().reshape(img, 128).astype(BF)
    r_slot = flag(iota((8 * groups, img), 0) == 8 * t_row + k_row).astype(BF)
    ximg[...] = mm(r_slot, vals).reshape(groups, 8, 128).astype(BF)
    spread(ximg, rimg, 2, False)
    red_t.middle()

    swap.wait_recv()
    for n in range(0, width, 256):
        w_rows = wv_v[n : n + 256, :]
        d = mm_nt(chalf[0], w_rows[:, :half_kv]) + mm_nt(chalf[1], w_rows[:, half_kv:])
        emb_acc[:, n : n + 256] = d
    d_img = emb_acc[...].astype(BF)
    for i in range(parts):
        res = mm_nt(d_img, wp_v[i * kchunk : (i + 1) * kchunk, :])
        for t in range(tps):
            gpf[t % 2, t // 2, :, i * kchunk : (i + 1) * kchunk] = res[8 * t : 8 * t + 8]
    red_g.start_pair()

    collected(rmeta, a_recv.at[1], groups - 1)
    rmeta[pl.ds(grp, 1)] = xmeta[...][None]
    metas = rmeta[...].reshape(8 * groups, 128).astype(BF)
    e_i, e_l = iota((groups, 8 * groups), 0), iota((groups, 8 * groups), 1)
    c_mat = mm(flag(e_l == 8 * e_i).astype(BF), metas)
    m_mat = mm(flag(e_l == 8 * e_i + 1).astype(BF), metas)
    s_mat = mm(flag(e_l == 8 * e_i + 2).astype(BF), metas)
    fan = flag(iota((groups, slots), 1) // cap == iota((groups, slots), 0)).astype(BF)
    used = lax.dot_general(
        c_mat.astype(BF), fan, (((0,), (0,)), ((), ())), preferred_element_type=F32
    )[:groups]
    k_of = (iota((groups, slots), 1) % cap).astype(F32)
    lost = jnp.sum(jnp.where(k_of < used, m_mat, 0.0)).reshape(1, 1)
    total = jnp.sum(s_mat[:, 0:1]).reshape(1, 1) - lost
    tot_s[...] = jnp.broadcast_to(total, (8, 128))
    tot_copies = []
    for i in range(1, pps):
        tot_copies.append(
            pltpu.make_async_remote_copy(
                tot_s, tot_r.at[i - 1], p_send.at[i - 1], p_recv.at[i - 1],
                device_id={"pp": lax.rem(pp + i, pps)}, device_id_type=MESH,
            )
        )
        tot_copies[-1].start()
    red_g.begin()

    x_l, x_i = iota((slots, 8 * groups), 1), iota((slots, 8 * groups), 0)
    holds = (x_i == cap * (x_l // 8) + x_l % 8) & (x_l % 8 < cap)
    sp8 = jnp.sum(jnp.where(holds, sp_col + 1, 0), axis=0, keepdims=True) - 1
    c_me = jnp.sum(jnp.where(iota((groups, 128), 1) == grp, c_mat, 0.0), axis=1, keepdims=True)
    c8 = jnp.sum(jnp.where(e_l // 8 == e_i, c_me, 0.0), axis=0, keepdims=True)
    valid = (iota((1, 8 * groups), 1) % 8).astype(F32) < c8
    pos8 = jnp.where(valid, sp8, -1)
    collected(rimg, a_recv.at[2], groups - 1)
    rimg[pl.ds(grp, 1)] = ximg[pl.ds(grp, 1)]
    put = flag(iota((seq, 8 * groups), 0) == pos8).astype(BF)
    zs[...] = mm(put, rimg[...].astype(F32).reshape(8 * groups, 128).astype(BF)).astype(BF).reshape(tps, rows_out, 128)
    z_copies = []
    for i in range(1, tps):
        peer = lax.rem(tp + i, tps)
        z_copies.append(
            pltpu.make_async_remote_copy(
                zs.at[peer], zr.at[tp], z_send.at[i - 1], z_recv.at[i - 1], device_id={"tp": peer}, device_id_type=MESH
            )
        )
        z_copies[-1].start()

    red_g.middle()
    text_vals = red_t.end().reshape(rows_out, kvd)
    is_img = jnp.sum(flag(iota((rows_out, 8 * groups), 0) + rows_out * tp == pos8), axis=1, keepdims=True)
    for c in z_copies:
        c.wait_recv()
    zr[pl.ds(tp, 1)] = zs[pl.ds(tp, 1)]
    for t in range(tps):
        cols = slice(128 * t, 128 * t + 128)
        values_out[:, cols] = jnp.where(is_img > 0.5, zr[t].astype(F32), text_vals[:, cols]).astype(BF)

    for c in tot_copies:
        c.wait_recv()
    text_total = tot_s[...]
    for i in range(1, pps):
        text_total = text_total + tot_r[i - 1]
    scale = (jnp.full((8, 128), float(pps * groups * seq), F32) / text_total)[:, 0:1]
    grad_out[...] = (red_g.end() * scale).astype(BF)

    for r in (red_i, red_t, red_g):
        r.drain()
    collected(xcot, a_send.at[0], groups - 1)
    collected(rmeta, a_send.at[1], groups - 1)
    collected(ximg, a_send.at[2], groups - 1)
    swap.wait_send()
    for c in z_copies + tot_copies:
        c.wait_send()


def body(vision, text_embed, target, slot_place, loss_mask, w_proj, w_value, cotangent):
    groups, tps, pps = lax.axis_size("grp"), lax.axis_size("tp"), lax.axis_size("pp")
    img, dvis, width = vision.shape[1], vision.shape[2], w_proj.shape[1]
    seq, kvd, slots = text_embed.shape[1], w_value.shape[1], slot_place.shape[2]
    chips, parts = tps // 2, 5
    rows, grows = seq // tps, img // tps
    vm = pltpu.VMEM
    dma = lambda *s: pltpu.SemaphoreType.DMA(s)

    def reduce_bufs(chunk):
        return [
            vm((2, chips) + chunk, F32), vm((chips,) + chunk, BF), vm((chips,) + chunk, BF), vm((chips,) + chunk, BF),
            vm(chunk, BF), vm(chunk, BF), vm(chunk, BF),
        ]

    scratch = (
        [vm((1, img), I32), vm((1, slots), I32), vm((1, seq), I32), vm((img, dvis), BF), vm((dvis, width), BF),
         vm((width, kvd), BF), vm((seq, width), BF), vm((seq, kvd // 2), BF), vm((img, width), F32)]
        + reduce_bufs((2, rows // 2, kvd))
        + reduce_bufs((2, img // 2, 128))
        + reduce_bufs((grows, dvis))
        + [vm((groups, 16, 128), BF), vm((groups, 16, 128), BF), vm((8, 128), F32), vm((groups, 8, 128), F32),
           vm((groups, 8, 128), BF), vm((groups, 8, 128), BF), vm((2, img, kvd // 2), BF),
           vm((tps, rows, 128), BF), vm((tps, rows, 128), BF), vm((8, 128), F32), vm((pps - 1, 8, 128), F32)]
        + [dma(7 + parts), dma(7), dma(7), dma(7), dma(7), dma(7), dma(7), dma(3), dma(3),
           dma(tps - 1), dma(tps - 1), dma(2), dma(pps - 1), dma(pps - 1)]
    )
    values, grads = pl.pallas_call(
        functools.partial(kernel, (groups, tps, pps, parts)),
        out_shape=(
            jax.ShapeDtypeStruct((rows, kvd), BF),
            jax.ShapeDtypeStruct((grows, dvis), BF),
        ),
        in_specs=[pl.BlockSpec(memory_space=pl.ANY)] * 8,
        out_specs=(pl.BlockSpec(memory_space=pltpu.VMEM), pl.BlockSpec(memory_space=pltpu.VMEM)),
        scratch_shapes=scratch,
        compiler_params=pltpu.CompilerParams(
            collective_id=0, has_side_effects=True, vmem_limit_bytes=48 * 1024 * 1024
        ),
    )(
        target.reshape(1, img), slot_place.reshape(1, slots), loss_mask, vision, w_proj, w_value, text_embed, cotangent
    )
    return values[None], grads[None]


def solution(mesh):
    in_specs = (
        P("pp", "grp", None),
        P("pp", "grp", "tp"),
        P("pp", "grp", None),
        P("pp", "grp", None),
        P("pp", "grp"),
        P(None, "tp"),
        P("tp", None),
        P("pp", "grp", None),
    )
    out_specs = (P("pp", ("grp", "tp"), None), P("pp", ("grp", "tp"), None))
    return jax.shard_map(body, mesh=mesh, in_specs=in_specs, out_specs=out_specs, check_vma=False)
```

```python
import functools

import jax
import jax.numpy as jnp
from jax import lax
from jax.experimental import pallas as pl
from jax.experimental.pallas import tpu as pltpu
from jax.sharding import PartitionSpec as P

MESH = pl.DeviceIdType.MESH
BF, F32, I32 = jnp.bfloat16, jnp.float32, jnp.int32


def iota(shape, dim):
    return lax.broadcasted_iota(I32, shape, dim)


def mm(a, b):
    return jnp.dot(a, b, preferred_element_type=F32)


def mm_nt(a, b):
    return lax.dot_general(a, b, (((1,), (1,)), ((), ())), preferred_element_type=F32)


def flag(cond):
    return jnp.where(cond, 1.0, 0.0).astype(F32)


def to_col(row):
    n = row.shape[1]
    return jnp.sum(jnp.where(iota((n, n), 0) == iota((n, n), 1), row, 0), axis=1, keepdims=True)


class Reduce:
    def __init__(self, env, half, pf, pb, pr, sb, r1, fdn, fup, send, recv):
        self.env, self.half = env, half
        self.pf, self.pb, self.pr, self.sb = pf, pb, pr, sb
        self.mine = pf.at[env["core"]]
        h_up, h_dn, h_op = env["h_up"], env["h_dn"], env["h_op"]
        own = lambda h, s: half(sb.at[h], s)
        table = [
            (own(h_op, 0), half(r1, 0), "up"),
            (own(h_op, 1), half(r1, 1), "dn"),
            (own(h_dn, 0), half(fup, 0), "dn"),
            (own(h_up, 1), half(fdn, 1), "up"),
            (own(h_up, 0), half(fdn, 0), "up"),
            (own(h_dn, 1), half(fup, 1), "dn"),
            (half(pb, 0), half(pr, 0), "partner"),
            (half(pb, 1), half(pr, 1), "partner"),
        ]
        self.copies = [
            pltpu.make_async_remote_copy(
                src, dst, send.at[i], recv.at[i], device_id={"tp": env[way]}, device_id_type=MESH
            )
            for i, (src, dst, way) in enumerate(table)
        ]
        self.r1, self.fdn, self.fup = r1, fdn, fup

    def start_pair(self, s):
        half = self.half
        half(self.pb, s)[...] = half(self.pf.at[1 - self.env["core"]], s)[...].astype(BF)
        self.copies[6 + s].start()

    def pair_sum(self, h, s):
        half = self.half
        return half(self.mine.at[h], s)[...] + half(self.pr.at[h], s)[...].astype(F32)

    def first(self, s):
        h = self.env["h_op"]
        self.copies[6 + s].wait_recv()
        self.half(self.sb.at[h], s)[...] = self.pair_sum(h, s).astype(BF)
        self.copies[s].start()

    def direct(self, s):
        h = self.env["h_dn" if s == 0 else "h_up"]
        self.half(self.sb.at[h], s)[...] = self.pair_sum(h, s).astype(BF)
        self.copies[2 + s].start()

    def relay(self, s):
        h = self.env["h_up" if s == 0 else "h_dn"]
        v = self.pair_sum(h, s)
        self.copies[s].wait_recv()
        self.half(self.sb.at[h], s)[...] = (v + self.half(self.r1, s)[...].astype(F32)).astype(BF)
        self.copies[4 + s].start()

    def end(self):
        env = self.env
        for i in (2, 3, 4, 5):
            self.copies[i].wait_recv()
        return (
            self.mine[env["hi"]]
            + self.pr[env["hi"]].astype(F32)
            + self.fdn[...].astype(F32)
            + self.fup[...].astype(F32)
        )

    def drain(self):
        for c in self.copies:
            c.wait_send()


def kernel(
    sizes, target, place, loss, vision, w_proj, w_value, text, cot, values_out, grad_out,
    target_v, place_v, loss_v, vision_v, wp_v, wv_v, text_v, cot_v,
    emb_acc, tpf, tpb, tpr, tsb, tr1, tfd, tfu,
    ipf, ipb, ipr, isb, ir1, ifd, ifu,
    gpf, gpb, gpr, gsb, gr1, gfd, gfu,
    xcot, rcot, xmeta, rmeta, ximg, rimg, chalf, zs, zr, tot_s, tot_r,
    load_sem, t_send, t_recv, i_send, i_recv, g_send, g_recv, a_send, a_recv, z_send, z_recv, s_sem, p_send, p_recv,
):
    groups, tps, pps, parts, cut = sizes
    grp, tp, pp = lax.axis_index("grp"), lax.axis_index("tp"), lax.axis_index("pp")
    core, hi = lax.rem(tp, 2), tp // 2
    chips = tps // 2
    env = dict(
        core=core, hi=hi, partner=tp + 1 - 2 * core,
        up=lax.rem(tp + 2, tps), dn=lax.rem(tp + tps - 2, tps),
        h_up=lax.rem(hi + 1, chips), h_dn=lax.rem(hi + chips - 1, chips), h_op=lax.rem(hi + 2, chips),
    )
    img, width = vision_v.shape[0], wp_v.shape[1]
    dvis, seq, kvd = wp_v.shape[0], text_v.shape[0], wv_v.shape[1]
    half_kv = kvd // 2
    slots = place_v.shape[1]
    cap = slots // groups
    kchunk = dvis // parts

    gx, gy = 4, groups // 4
    offsets = [(dx, dy) for dx in range(gx) for dy in range(gy) if dx or dy]
    offsets.sort(key=lambda o: -(min(o[0], gx - o[0]) + min(o[1], gy - o[1])))
    px, py = grp // gy, lax.rem(grp, gy)
    peers = [lax.rem(px + dx, gx) * gy + lax.rem(py + dy, gy) for dx, dy in offsets]

    pairs = [
        (place, place_v), (target, target_v), (loss, loss_v),
        (cot.at[0, :, pl.ds(pl.multiple_of(core * half_kv, 128), half_kv)], cot_v), (vision.at[0], vision_v),
    ] + [(w_proj.at[pl.ds(i * kchunk, kchunk)], wp_v.at[pl.ds(i * kchunk, kchunk)]) for i in range(parts)]
    pairs += [(w_value, wv_v), (text.at[0], text_v)]
    loads = [pltpu.make_async_copy(s, d, load_sem.at[i]) for i, (s, d) in enumerate(pairs)]
    for c in loads:
        c.start()
    l_cot, l_vision, l_proj, l_value, l_text = loads[3], loads[4], loads[5:-2], loads[-2], loads[-1]
    barrier = pltpu.get_barrier_semaphore()
    for p in peers:
        pl.semaphore_signal(barrier, inc=1, device_id={"grp": p}, device_id_type=MESH)
    for i in range(1, tps):
        pl.semaphore_signal(barrier, inc=1, device_id={"tp": lax.rem(tp + i, tps)}, device_id_type=MESH)
    for i in range(1, pps):
        pl.semaphore_signal(barrier, inc=1, device_id={"pp": lax.rem(pp + i, pps)}, device_id_type=MESH)

    for c in loads[:3]:
        c.wait()
    t_row = target_v[...]
    t_col = to_col(t_row)
    same = t_col == t_row
    k_col = jnp.sum(jnp.where(same & (iota((img, img), 1) < iota((img, img), 0)), 1, 0), axis=1, keepdims=True)
    k_row = jnp.sum(jnp.where(same & (iota((img, img), 0) < iota((img, img), 1)), 1, 0), axis=0, keepdims=True)
    counts = jnp.sum(flag(t_col == iota((img, 128), 1)), axis=0, keepdims=True)
    sp_row = place_v[...]
    sp_col = to_col(sp_row)
    loss_f = loss_v[...].astype(F32)
    at_slot = flag(sp_col == iota((slots, seq), 1))
    mask_slot = jnp.sum(at_slot * loss_f, axis=1, keepdims=True)
    eye = iota((slots, slots), 0) == iota((slots, slots), 1)
    mask_row = jnp.sum(jnp.where(eye, mask_slot, 0.0), axis=0, keepdims=True)
    mask_sum = jnp.sum(loss_f, axis=1, keepdims=True)
    r8 = iota((8, 128), 0)
    meta = jnp.where(r8 == 0, counts, jnp.where(r8 == 1, mask_row, jnp.where(r8 == 2, mask_sum, 0.0)))
    xmeta[...] = meta

    d_i, d_l = iota((4 * slots, 4 * slots), 0), iota((4 * slots, 4 * slots), 1)
    shuffle = flag(d_l == slots * ((d_i // 4) % 4) + 4 * (d_i // 16) + d_i % 4).astype(BF)
    l_cot.wait()
    y = mm(at_slot.astype(BF), cot_v[...]).astype(BF)
    ystack = jnp.concatenate([y[:, 128 * j : 128 * (j + 1)] for j in range(4)], axis=0)
    xcot[...] = mm(shuffle, ystack).astype(BF).reshape(groups, 16, 128)

    l_vision.wait()
    for i in range(parts):
        l_proj[i].wait()
        part = mm(vision_v[:, i * kchunk : (i + 1) * kchunk], wp_v[i * kchunk : (i + 1) * kchunk, :])
        if i == 0:
            emb_acc[...] = part
        else:
            emb_acc[...] += part
    l_value.wait()
    emb = emb_acc[...].astype(BF)
    for t in range(tps):
        if t % 2 == 0:
            res = mm(emb, wv_v[:, 128 * t : 128 * t + 256])
        piece = res[:, 128 * (t % 2) : 128 * (t % 2) + 128]
        for s in range(2):
            ipf[t % 2, t // 2, s] = piece[s * (img // 2) : (s + 1) * (img // 2)]

    lead = lambda ref, s: ref.at[..., s, :, :] if len(ref.shape) == 4 else ref.at[s]
    span = (pl.ds(0, cut), pl.ds(cut, dvis - cut))
    lane_cut = lambda ref, s: ref.at[..., span[s]]
    red_i = Reduce(env, lead, ipf, ipb, ipr, isb, ir1, ifd, ifu, i_send, i_recv)
    red_t = Reduce(env, lead, tpf, tpb, tpr, tsb, tr1, tfd, tfu, t_send, t_recv)
    red_g = Reduce(env, lane_cut, gpf, gpb, gpr, gsb, gr1, gfd, gfu, g_send, g_recv)

    pl.semaphore_wait(barrier, (tps - 1) + (groups - 1) + (pps - 1))

    red_i.start_pair(0)
    red_i.start_pair(1)

    def spread(src, dst, k, whole):
        for p in peers:
            pltpu.make_async_remote_copy(
                src if whole else src.at[p], dst.at[grp], a_send.at[k], a_recv.at[k],
                device_id={"grp": p}, device_id_type=MESH,
            ).start()

    def collected(ref, sem, n):
        pltpu.make_async_copy(ref.at[pl.ds(0, n)], ref.at[pl.ds(0, n)], sem).wait()

    spread(xcot, rcot, 0, False)

    l_text.wait()
    rows_out = seq // tps
    hr = rows_out // 2
    for n in range(4):
        cols = pl.ds(n * 256, 256)
        res = mm(text_v[...], wv_v[:, cols])
        for t in range(tps):
            for s in range(2):
                r0 = t * rows_out + s * hr
                tpf[t % 2, t // 2, s, :, cols] = res[r0 : r0 + hr]

    red_i.first(0)
    red_i.first(1)
    red_i.direct(0)
    red_i.direct(1)
    red_t.start_pair(0)
    red_t.start_pair(1)
    spread(xmeta, rmeta, 1, True)
    red_t.first(0)
    red_t.first(1)
    red_i.relay(0)
    red_i.relay(1)
    red_t.direct(0)
    red_t.direct(1)

    lane = iota((img, 4 * slots), 1)
    pick = jnp.concatenate(
        [flag(lane == 16 * t_col + 4 * j + k_col).astype(BF) for j in range(4)], axis=0
    )
    collected(rcot, a_recv.at[0], groups - 1)
    rcot[pl.ds(grp, 1)] = xcot[pl.ds(grp, 1)]
    got = mm(pick, rcot[...].reshape(4 * slots, 128)).astype(BF)
    mine = jnp.concatenate([got[img * j : img * (j + 1)] for j in range(4)], axis=1)
    chalf[pl.ds(core, 1)] = mine[None]
    swap = pltpu.make_async_remote_copy(
        chalf.at[core], chalf.at[core], s_sem.at[0], s_sem.at[1], device_id={"tp": env["partner"]}, device_id_type=MESH
    )
    swap.start()

    half_cols = lambda c: pl.ds(pl.multiple_of(c * half_kv, 128), half_kv)
    for n in range(0, width, 256):
        emb_acc[:, n : n + 256] = mm_nt(mine, wv_v[n : n + 256, half_cols(core)])
    red_t.relay(0)
    red_t.relay(1)
    swap.wait_recv()
    other = chalf[1 - core]
    for n in range(0, width, 256):
        emb_acc[:, n : n + 256] += mm_nt(other, wv_v[n : n + 256, half_cols(1 - core)])
    d_img = emb_acc[...].astype(BF)

    vals = red_i.end().reshape(img, 128).astype(BF)
    r_slot = flag(iota((8 * groups, img), 0) == 8 * t_row + k_row).astype(BF)
    ximg[...] = mm(r_slot, vals).reshape(groups, 8, 128).astype(BF)
    spread(ximg, rimg, 2, False)

    for s, bounds in enumerate(((0, cut // 2, cut), (cut, cut + (dvis - cut) // 256 * 128, dvis))):
        for lo, up in zip(bounds[:-1], bounds[1:]):
            res = mm_nt(d_img, wp_v[lo:up, :])
            for t in range(tps):
                gpf[t % 2, t // 2, :, lo:up] = res[8 * t : 8 * t + 8]
        red_g.start_pair(s)
    red_g.first(0)

    collected(rmeta, a_recv.at[1], groups - 1)
    rmeta[pl.ds(grp, 1)] = xmeta[...][None]
    metas = rmeta[...].reshape(8 * groups, 128).astype(BF)
    e_i, e_l = iota((groups, 8 * groups), 0), iota((groups, 8 * groups), 1)
    c_mat = mm(flag(e_l == 8 * e_i).astype(BF), metas)
    m_mat = mm(flag(e_l == 8 * e_i + 1).astype(BF), metas)
    s_mat = mm(flag(e_l == 8 * e_i + 2).astype(BF), metas)
    fan = flag(iota((groups, slots), 1) // cap == iota((groups, slots), 0)).astype(BF)
    used = lax.dot_general(
        c_mat.astype(BF), fan, (((0,), (0,)), ((), ())), preferred_element_type=F32
    )[:groups]
    k_of = (iota((groups, slots), 1) % cap).astype(F32)
    lost = jnp.sum(jnp.where(k_of < used, m_mat, 0.0)).reshape(1, 1)
    total = jnp.sum(s_mat[:, 0:1]).reshape(1, 1) - lost
    tot_s[...] = jnp.broadcast_to(total, (8, 128))
    tot_copies = []
    for i in range(1, pps):
        tot_copies.append(
            pltpu.make_async_remote_copy(
                tot_s, tot_r.at[i - 1], p_send.at[i - 1], p_recv.at[i - 1],
                device_id={"pp": lax.rem(pp + i, pps)}, device_id_type=MESH,
            )
        )
    red_g.first(1)
    for c in tot_copies:
        c.start()
    red_g.direct(0)
    red_g.direct(1)

    x_l, x_i = iota((slots, 8 * groups), 1), iota((slots, 8 * groups), 0)
    holds = (x_i == cap * (x_l // 8) + x_l % 8) & (x_l % 8 < cap)
    sp8 = jnp.sum(jnp.where(holds, sp_col + 1, 0), axis=0, keepdims=True) - 1
    c_me = jnp.sum(jnp.where(iota((groups, 128), 1) == grp, c_mat, 0.0), axis=1, keepdims=True)
    c8 = jnp.sum(jnp.where(e_l // 8 == e_i, c_me, 0.0), axis=0, keepdims=True)
    valid = (iota((1, 8 * groups), 1) % 8).astype(F32) < c8
    pos8 = jnp.where(valid, sp8, -1)
    put = flag(iota((seq, 8 * groups), 0) == pos8).astype(BF)
    collected(rimg, a_recv.at[2], groups - 1)
    rimg[pl.ds(grp, 1)] = ximg[pl.ds(grp, 1)]
    zs[...] = mm(put, rimg[...].astype(F32).reshape(8 * groups, 128).astype(BF)).astype(BF).reshape(tps, rows_out, 128)
    z_copies = []
    for i in (4, 3, 5, 2, 6, 1, 7):
        peer = lax.rem(tp + i, tps)
        z_copies.append(
            pltpu.make_async_remote_copy(
                zs.at[peer], zr.at[tp], z_send.at[i - 1], z_recv.at[i - 1], device_id={"tp": peer}, device_id_type=MESH
            )
        )
        z_copies[-1].start()

    red_g.relay(0)
    red_g.relay(1)
    text_vals = red_t.end().reshape(rows_out, kvd)
    is_img = jnp.sum(flag(iota((rows_out, 8 * groups), 0) + rows_out * tp == pos8), axis=1, keepdims=True)
    for c in z_copies:
        c.wait_recv()
    zr[pl.ds(tp, 1)] = zs[pl.ds(tp, 1)]
    for t in range(tps):
        cols = slice(128 * t, 128 * t + 128)
        values_out[:, cols] = jnp.where(is_img > 0.5, zr[t].astype(F32), text_vals[:, cols]).astype(BF)

    for c in tot_copies:
        c.wait_recv()
    text_total = tot_s[...]
    for i in range(1, pps):
        text_total = text_total + tot_r[i - 1]
    scale = (jnp.full((8, 128), float(pps * groups * seq), F32) / text_total)[:, 0:1]
    grad_out[...] = (red_g.end() * scale).astype(BF)

    for r in (red_i, red_t, red_g):
        r.drain()
    collected(xcot, a_send.at[0], groups - 1)
    collected(rmeta, a_send.at[1], groups - 1)
    collected(ximg, a_send.at[2], groups - 1)
    swap.wait_send()
    for c in z_copies + tot_copies:
        c.wait_send()


def body(vision, text_embed, target, slot_place, loss_mask, w_proj, w_value, cotangent):
    groups, tps, pps = lax.axis_size("grp"), lax.axis_size("tp"), lax.axis_size("pp")
    img, dvis, width = vision.shape[1], vision.shape[2], w_proj.shape[1]
    seq, kvd, slots = text_embed.shape[1], w_value.shape[1], slot_place.shape[2]
    chips, parts = tps // 2, 5
    cut = dvis // 256 * 128
    rows, grows = seq // tps, img // tps
    vm = pltpu.VMEM
    dma = lambda *s: pltpu.SemaphoreType.DMA(s)

    def reduce_bufs(chunk):
        return [
            vm((2, chips) + chunk, F32), vm((chips,) + chunk, BF), vm((chips,) + chunk, BF), vm((chips,) + chunk, BF),
            vm(chunk, BF), vm(chunk, BF), vm(chunk, BF),
        ]

    scratch = (
        [vm((1, img), I32), vm((1, slots), I32), vm((1, seq), I32), vm((img, dvis), BF), vm((dvis, width), BF),
         vm((width, kvd), BF), vm((seq, width), BF), vm((seq, kvd // 2), BF), vm((img, width), F32)]
        + reduce_bufs((2, rows // 2, kvd))
        + reduce_bufs((2, img // 2, 128))
        + reduce_bufs((grows, dvis))
        + [vm((groups, 16, 128), BF), vm((groups, 16, 128), BF), vm((8, 128), F32), vm((groups, 8, 128), F32),
           vm((groups, 8, 128), BF), vm((groups, 8, 128), BF), vm((2, img, kvd // 2), BF),
           vm((tps, rows, 128), BF), vm((tps, rows, 128), BF), vm((8, 128), F32), vm((pps - 1, 8, 128), F32)]
        + [dma(7 + parts), dma(8), dma(8), dma(8), dma(8), dma(8), dma(8), dma(3), dma(3),
           dma(tps - 1), dma(tps - 1), dma(2), dma(pps - 1), dma(pps - 1)]
    )
    in_hbm = lambda a: pltpu.with_memory_space_constraint(a, pltpu.HBM)
    values, grads = pl.pallas_call(
        functools.partial(kernel, (groups, tps, pps, parts, cut)),
        out_shape=(
            jax.ShapeDtypeStruct((rows, kvd), BF),
            jax.ShapeDtypeStruct((grows, dvis), BF),
        ),
        in_specs=[pl.BlockSpec(memory_space=pl.ANY)] * 8,
        out_specs=(pl.BlockSpec(memory_space=pltpu.VMEM), pl.BlockSpec(memory_space=pltpu.VMEM)),
        scratch_shapes=scratch,
        compiler_params=pltpu.CompilerParams(
            collective_id=0, has_side_effects=True, vmem_limit_bytes=48 * 1024 * 1024
        ),
    )(
        *map(
            in_hbm,
            (target.reshape(1, img), slot_place.reshape(1, slots), loss_mask, vision, w_proj, w_value, text_embed, cotangent),
        )
    )
    return values[None], grads[None]


def solution(mesh):
    in_specs = (
        P("pp", "grp", None),
        P("pp", "grp", "tp"),
        P("pp", "grp", None),
        P("pp", "grp", None),
        P("pp", "grp"),
        P(None, "tp"),
        P("tp", None),
        P("pp", "grp", None),
    )
    out_specs = (P("pp", ("grp", "tp"), None), P("pp", ("grp", "tp"), None))
    return jax.shard_map(body, mesh=mesh, in_specs=in_specs, out_specs=out_specs, check_vma=False)
```

```python
import functools

import jax
import jax.numpy as jnp
from jax import lax
from jax.experimental import pallas as pl
from jax.experimental.pallas import tpu as pltpu
from jax.sharding import PartitionSpec as P

MESH = pl.DeviceIdType.MESH
BF, F32, I32 = jnp.bfloat16, jnp.float32, jnp.int32


def iota(shape, dim):
    return lax.broadcasted_iota(I32, shape, dim)


def mm(a, b):
    return jnp.dot(a, b, preferred_element_type=F32)


def mm_nt(a, b):
    return lax.dot_general(a, b, (((1,), (1,)), ((), ())), preferred_element_type=F32)


def flag(cond):
    return jnp.where(cond, 1.0, 0.0).astype(F32)


def to_col(row):
    n = row.shape[1]
    return jnp.sum(jnp.where(iota((n, n), 0) == iota((n, n), 1), row, 0), axis=1, keepdims=True)


def collected(ref, sem, n):
    pltpu.make_async_copy(ref.at[pl.ds(0, n)], ref.at[pl.ds(0, n)], sem).wait()


class Reduce:
    def __init__(self, env, half, pf, pb, pr, sb, r1, fdn, fup, send, recv):
        self.env, self.half = env, half
        self.pf, self.pb, self.pr, self.sb = pf, pb, pr, sb
        self.mine = pf.at[env["core"]]
        h_up, h_dn, h_op = env["h_up"], env["h_dn"], env["h_op"]
        own = lambda h, s: half(sb.at[h], s)
        table = [
            (own(h_op, 0), half(r1, 0), "up"),
            (own(h_op, 1), half(r1, 1), "dn"),
            (own(h_dn, 0), half(fup, 0), "dn"),
            (own(h_up, 1), half(fdn, 1), "up"),
            (own(h_up, 0), half(fdn, 0), "up"),
            (own(h_dn, 1), half(fup, 1), "dn"),
            (half(pb, 0), half(pr, 0), "partner"),
            (half(pb, 1), half(pr, 1), "partner"),
        ]
        self.copies = [
            pltpu.make_async_remote_copy(
                src, dst, send.at[1 if i > 5 else 0], recv.at[i if i < 2 else 2 if i < 6 else i - 3],
                device_id={"tp": env[way]}, device_id_type=MESH,
            )
            for i, (src, dst, way) in enumerate(table)
        ]
        self.r1, self.fdn, self.fup, self.send, self.recv = r1, fdn, fup, send, recv

    def start_pair(self, s):
        half = self.half
        half(self.pb, s)[...] = half(self.pf.at[1 - self.env["core"]], s)[...].astype(BF)
        self.copies[6 + s].start()

    def pair_sum(self, h, s):
        half = self.half
        return half(self.mine.at[h], s)[...] + half(self.pr.at[h], s)[...].astype(F32)

    def first(self, s):
        h = self.env["h_op"]
        self.copies[6 + s].wait_recv()
        self.half(self.sb.at[h], s)[...] = self.pair_sum(h, s).astype(BF)
        self.copies[s].start()

    def direct(self, s):
        h = self.env["h_dn" if s == 0 else "h_up"]
        self.half(self.sb.at[h], s)[...] = self.pair_sum(h, s).astype(BF)
        self.copies[2 + s].start()

    def relay(self, s):
        h = self.env["h_up" if s == 0 else "h_dn"]
        v = self.pair_sum(h, s)
        self.copies[s].wait_recv()
        self.half(self.sb.at[h], s)[...] = (v + self.half(self.r1, s)[...].astype(F32)).astype(BF)
        self.copies[4 + s].start()

    def end(self):
        env = self.env
        collected(self.pr, self.recv.at[2], 2)
        return (
            self.mine[env["hi"]]
            + self.pr[env["hi"]].astype(F32)
            + self.fdn[...].astype(F32)
            + self.fup[...].astype(F32)
        )

    def drain(self):
        collected(self.pb, self.send.at[1], self.pb.shape[0])
        collected(self.sb, self.send.at[0], 3)


def kernel(
    sizes, target, place, loss, vision, w_proj, w_value, text, cot, values_out, grad_out,
    target_v, place_v, loss_v, vision_v, wp_v, wv_v, text_v, cot_v,
    emb_acc, tpf, tpb, tpr, tsb, tr1, tfd, tfu,
    ipf, ipb, ipr, isb, ir1, ifd, ifu,
    gpf, gpb, gpr, gsb, gr1, gfd, gfu,
    xcot, rcot, xmeta, rmeta, ximg, rimg, chalf, zs, zr, tot_s, tot_r,
    load_sem, t_send, t_recv, i_send, i_recv, g_send, g_recv, a_send, a_recv, z_send, z_recv, s_sem, p_send, p_recv,
):
    groups, tps, pps, parts, cut = sizes
    grp, tp, pp = lax.axis_index("grp"), lax.axis_index("tp"), lax.axis_index("pp")
    core, hi = lax.rem(tp, 2), tp // 2
    chips = tps // 2
    env = dict(
        core=core, hi=hi, partner=tp + 1 - 2 * core,
        up=lax.rem(tp + 2, tps), dn=lax.rem(tp + tps - 2, tps),
        h_up=lax.rem(hi + 1, chips), h_dn=lax.rem(hi + chips - 1, chips), h_op=lax.rem(hi + 2, chips),
    )
    img, width = vision_v.shape[0], wp_v.shape[1]
    dvis, seq, kvd = wp_v.shape[0], text_v.shape[0], wv_v.shape[1]
    half_kv = kvd // 2
    slots = place_v.shape[1]
    cap = slots // groups
    kchunk = dvis // parts

    gx, gy = 4, groups // 4
    offsets = [(dx, dy) for dx in range(gx) for dy in range(gy) if dx or dy]
    offsets.sort(key=lambda o: -(min(o[0], gx - o[0]) + min(o[1], gy - o[1])))
    px, py = grp // gy, lax.rem(grp, gy)
    peers = [lax.rem(px + dx, gx) * gy + lax.rem(py + dy, gy) for dx, dy in offsets]

    pairs = [
        (place, place_v), (target, target_v), (loss, loss_v),
        (cot.at[0, :, pl.ds(pl.multiple_of(core * half_kv, 128), half_kv)], cot_v), (vision.at[0], vision_v),
    ] + [(w_proj.at[pl.ds(i * kchunk, kchunk)], wp_v.at[pl.ds(i * kchunk, kchunk)]) for i in range(parts)]
    pairs += [(w_value, wv_v), (text.at[0], text_v)]
    loads = [pltpu.make_async_copy(s, d, load_sem.at[i]) for i, (s, d) in enumerate(pairs)]
    for c in loads[:4]:
        c.start()
    l_cot, l_vision, l_proj, l_value, l_text = loads[3], loads[4], loads[5:-2], loads[-2], loads[-1]
    barrier = pltpu.get_barrier_semaphore()
    for p in peers:
        pl.semaphore_signal(barrier, inc=1, device_id={"grp": p}, device_id_type=MESH)
    for c in loads[4:]:
        c.start()
    for i in range(1, tps):
        pl.semaphore_signal(barrier, inc=1, device_id={"tp": lax.rem(tp + i, tps)}, device_id_type=MESH)
    for i in range(1, pps):
        pl.semaphore_signal(barrier, inc=1, device_id={"pp": lax.rem(pp + i, pps)}, device_id_type=MESH)

    for c in loads[:3]:
        c.wait()
    t_row = target_v[...]
    t_col = to_col(t_row)
    same = t_col == t_row
    k_col = jnp.sum(jnp.where(same & (iota((img, img), 1) < iota((img, img), 0)), 1, 0), axis=1, keepdims=True)
    k_row = jnp.sum(jnp.where(same & (iota((img, img), 0) < iota((img, img), 1)), 1, 0), axis=0, keepdims=True)
    counts = jnp.sum(flag(t_col == iota((img, 128), 1)), axis=0, keepdims=True)
    sp_row = place_v[...]
    sp_col = to_col(sp_row)
    loss_f = loss_v[...].astype(F32)
    at_slot = flag(sp_col == iota((slots, seq), 1))
    mask_slot = jnp.sum(at_slot * loss_f, axis=1, keepdims=True)
    eye = iota((slots, slots), 0) == iota((slots, slots), 1)
    mask_row = jnp.sum(jnp.where(eye, mask_slot, 0.0), axis=0, keepdims=True)
    mask_sum = jnp.sum(loss_f, axis=1, keepdims=True)
    r8 = iota((8, 128), 0)
    meta = jnp.where(r8 == 0, counts, jnp.where(r8 == 1, mask_row, jnp.where(r8 == 2, mask_sum, 0.0)))
    xmeta[...] = meta

    d_i = iota((4 * slots, 1), 0)
    d_from = slots * ((d_i // 4) % 4) + 4 * (d_i // 16) + d_i % 4
    shuffle = flag(iota((4 * slots, 4 * slots), 1) == d_from).astype(BF)
    l_cot.wait()
    y = mm(at_slot.astype(BF), cot_v[...]).astype(BF)
    ystack = jnp.concatenate([y[:, 128 * j : 128 * (j + 1)] for j in range(4)], axis=0)
    xcot[...] = mm(shuffle, ystack).astype(BF).reshape(groups, 16, 128)

    l_vision.wait()
    for i in range(parts):
        l_proj[i].wait()
        part = mm(vision_v[:, i * kchunk : (i + 1) * kchunk], wp_v[i * kchunk : (i + 1) * kchunk, :])
        if i == 0:
            emb_acc[...] = part
        else:
            emb_acc[...] += part
    l_value.wait()
    emb = emb_acc[...].astype(BF)
    for t in range(tps):
        if t % 2 == 0:
            res = mm(emb, wv_v[:, 128 * t : 128 * t + 256])
        piece = res[:, 128 * (t % 2) : 128 * (t % 2) + 128]
        for s in range(2):
            ipf[t % 2, t // 2, s] = piece[s * (img // 2) : (s + 1) * (img // 2)]

    lead = lambda ref, s: ref.at[..., s, :, :] if len(ref.shape) == 4 else ref.at[s]
    span = (pl.ds(0, cut), pl.ds(cut, dvis - cut))
    lane_cut = lambda ref, s: ref.at[..., span[s]]
    red_i = Reduce(env, lead, ipf, ipb, ipr, isb, ir1, ifd, ifu, i_send, i_recv)
    red_t = Reduce(env, lead, tpf, tpb, tpr, tsb, tr1, tfd, tfu, t_send, t_recv)
    red_g = Reduce(env, lane_cut, gpf, gpb, gpr, gsb, gr1, gfd, gfu, g_send, g_recv)

    pl.semaphore_wait(barrier, (tps - 1) + (groups - 1) + (pps - 1))

    red_i.start_pair(0)
    red_i.start_pair(1)

    def spread(src, dst, k, whole):
        for p in peers:
            pltpu.make_async_remote_copy(
                src if whole else src.at[p], dst.at[grp], a_send.at[k], a_recv.at[k],
                device_id={"grp": p}, device_id_type=MESH,
            ).start()

    spread(xcot, rcot, 0, False)

    l_text.wait()
    rows_out = seq // tps
    hr = rows_out // 2
    for n in range(4):
        cols = pl.ds(n * 256, 256)
        res = mm(text_v[...], wv_v[:, cols])
        for t in range(tps):
            for s in range(2):
                r0 = t * rows_out + s * hr
                tpf[t % 2, t // 2, s, :, cols] = res[r0 : r0 + hr]

    red_i.first(0)
    red_i.first(1)
    red_i.direct(0)
    red_i.direct(1)
    red_t.start_pair(0)
    red_t.start_pair(1)
    spread(xmeta, rmeta, 1, True)
    red_t.first(0)
    red_t.first(1)
    red_i.relay(0)
    red_i.relay(1)
    red_t.direct(0)
    red_t.direct(1)

    lane = iota((img, 4 * slots), 1)
    pick = jnp.concatenate(
        [flag(lane == 16 * t_col + 4 * j + k_col).astype(BF) for j in range(4)], axis=0
    )
    collected(rcot, a_recv.at[0], groups - 1)
    rcot[pl.ds(grp, 1)] = xcot[pl.ds(grp, 1)]
    got = mm(pick, rcot[...].reshape(4 * slots, 128)).astype(BF)
    mine = jnp.concatenate([got[img * j : img * (j + 1)] for j in range(4)], axis=1)
    chalf[pl.ds(core, 1)] = mine[None]
    swap = pltpu.make_async_remote_copy(
        chalf.at[core], chalf.at[core], s_sem.at[0], s_sem.at[1], device_id={"tp": env["partner"]}, device_id_type=MESH
    )
    swap.start()

    half_cols = lambda c: pl.ds(pl.multiple_of(c * half_kv, 128), half_kv)
    for n in range(0, width, 256):
        emb_acc[:, n : n + 256] = mm_nt(mine, wv_v[n : n + 256, half_cols(core)])
    swap.wait_recv()
    red_t.relay(0)
    red_t.relay(1)
    other = chalf[1 - core]
    for n in range(0, width, 256):
        emb_acc[:, n : n + 256] += mm_nt(other, wv_v[n : n + 256, half_cols(1 - core)])
    d_img = emb_acc[...].astype(BF)

    def grad_part(lo, up):
        res = mm_nt(d_img, wp_v[lo:up, :])
        for t in range(tps):
            gpf[t % 2, t // 2, :, lo:up] = res[8 * t : 8 * t + 8]

    grad_part(0, cut // 2)
    grad_part(cut // 2, cut)
    red_g.start_pair(0)

    vals = red_i.end().reshape(img, 128).astype(BF)
    r_slot = flag(iota((8 * groups, img), 0) == 8 * t_row + k_row).astype(BF)
    ximg[...] = mm(r_slot, vals).reshape(groups, 8, 128).astype(BF)
    spread(ximg, rimg, 2, False)

    mid = cut + (dvis - cut) // 256 * 128
    grad_part(cut, mid)
    red_g.first(0)
    grad_part(mid, dvis)
    red_g.start_pair(1)

    collected(rmeta, a_recv.at[1], groups - 1)
    rmeta[pl.ds(grp, 1)] = xmeta[...][None]
    metas = rmeta[...].reshape(8 * groups, 128).astype(BF)
    e_i, e_l = iota((groups, 8 * groups), 0), iota((groups, 8 * groups), 1)
    c_mat = mm(flag(e_l == 8 * e_i).astype(BF), metas)
    m_mat = mm(flag(e_l == 8 * e_i + 1).astype(BF), metas)
    s_mat = mm(flag(e_l == 8 * e_i + 2).astype(BF), metas)
    fan = flag(iota((groups, slots), 1) // cap == iota((groups, slots), 0)).astype(BF)
    used = lax.dot_general(
        c_mat.astype(BF), fan, (((0,), (0,)), ((), ())), preferred_element_type=F32
    )[:groups]
    k_of = (iota((groups, slots), 1) % cap).astype(F32)
    lost = jnp.sum(jnp.where(k_of < used, m_mat, 0.0)).reshape(1, 1)
    total = jnp.sum(s_mat[:, 0:1]).reshape(1, 1) - lost
    tot_s[...] = jnp.broadcast_to(total, (8, 128))
    tot_copies = []
    for i in range(1, pps):
        tot_copies.append(
            pltpu.make_async_remote_copy(
                tot_s, tot_r.at[i - 1], p_send.at[0], p_recv.at[0],
                device_id={"pp": lax.rem(pp + i, pps)}, device_id_type=MESH,
            )
        )
    red_g.first(1)
    for c in tot_copies:
        c.start()
    red_g.direct(0)
    red_g.direct(1)

    x_l, x_i = iota((slots, 8 * groups), 1), iota((slots, 8 * groups), 0)
    holds = (x_i == cap * (x_l // 8) + x_l % 8) & (x_l % 8 < cap)
    sp8 = jnp.sum(jnp.where(holds, sp_col + 1, 0), axis=0, keepdims=True) - 1
    c_me = jnp.sum(jnp.where(iota((groups, 128), 1) == grp, c_mat, 0.0), axis=1, keepdims=True)
    c8 = jnp.sum(jnp.where(e_l // 8 == e_i, c_me, 0.0), axis=0, keepdims=True)
    valid = (iota((1, 8 * groups), 1) % 8).astype(F32) < c8
    pos8 = jnp.where(valid, sp8, -1)
    put = flag(iota((seq, 8 * groups), 0) == pos8).astype(BF)
    collected(rimg, a_recv.at[2], groups - 1)
    rimg[pl.ds(grp, 1)] = ximg[pl.ds(grp, 1)]
    zs[...] = mm(put, rimg[...].astype(F32).reshape(8 * groups, 128).astype(BF)).astype(BF).reshape(tps, rows_out, 128)
    z_copies = []
    for i in (4, 3, 5, 2, 6, 1, 7):
        peer = lax.rem(tp + i, tps)
        z_copies.append(
            pltpu.make_async_remote_copy(
                zs.at[peer], zr.at[tp], z_send.at[0], z_recv.at[0], device_id={"tp": peer}, device_id_type=MESH
            )
        )
        z_copies[-1].start()

    red_g.relay(0)
    red_g.relay(1)
    text_vals = red_t.end().reshape(rows_out, kvd)
    is_img = jnp.sum(flag(iota((rows_out, 8 * groups), 0) + rows_out * tp == pos8), axis=1, keepdims=True)
    collected(zr, z_recv.at[0], tps - 1)
    zr[pl.ds(tp, 1)] = zs[pl.ds(tp, 1)]
    for t in range(tps):
        cols = slice(128 * t, 128 * t + 128)
        values_out[:, cols] = jnp.where(is_img > 0.5, zr[t].astype(F32), text_vals[:, cols]).astype(BF)

    collected(tot_r, p_recv.at[0], pps - 1)
    text_total = tot_s[...]
    for i in range(1, pps):
        text_total = text_total + tot_r[i - 1]
    scale = (jnp.full((8, 128), float(pps * groups * seq), F32) / text_total)[:, 0:1]
    grad_out[...] = (red_g.end() * scale).astype(BF)

    for r in (red_i, red_t, red_g):
        r.drain()
    collected(xcot, a_send.at[0], groups - 1)
    collected(rmeta, a_send.at[1], groups - 1)
    collected(ximg, a_send.at[2], groups - 1)
    swap.wait_send()
    collected(zs, z_send.at[0], tps - 1)
    collected(tot_r, p_send.at[0], pps - 1)


def body(vision, text_embed, target, slot_place, loss_mask, w_proj, w_value, cotangent):
    groups, tps, pps = lax.axis_size("grp"), lax.axis_size("tp"), lax.axis_size("pp")
    img, dvis, width = vision.shape[1], vision.shape[2], w_proj.shape[1]
    seq, kvd, slots = text_embed.shape[1], w_value.shape[1], slot_place.shape[2]
    chips, parts = tps // 2, 5
    cut = dvis // 256 * 128
    rows, grows = seq // tps, img // tps
    vm = pltpu.VMEM
    dma = lambda *s: pltpu.SemaphoreType.DMA(s)

    def reduce_bufs(chunk):
        return [
            vm((2, chips) + chunk, F32), vm((chips,) + chunk, BF), vm((chips,) + chunk, BF), vm((chips,) + chunk, BF),
            vm(chunk, BF), vm(chunk, BF), vm(chunk, BF),
        ]

    scratch = (
        [vm((1, img), I32), vm((1, slots), I32), vm((1, seq), I32), vm((img, dvis), BF), vm((dvis, width), BF),
         vm((width, kvd), BF), vm((seq, width), BF), vm((seq, kvd // 2), BF), vm((img, width), F32)]
        + reduce_bufs((2, rows // 2, kvd))
        + reduce_bufs((2, img // 2, 128))
        + reduce_bufs((grows, dvis))
        + [vm((groups, 16, 128), BF), vm((groups, 16, 128), BF), vm((8, 128), F32), vm((groups, 8, 128), F32),
           vm((groups, 8, 128), BF), vm((groups, 8, 128), BF), vm((2, img, kvd // 2), BF),
           vm((tps, rows, 128), BF), vm((tps, rows, 128), BF), vm((8, 128), F32), vm((pps - 1, 8, 128), F32)]
        + [dma(7 + parts), dma(2), dma(5), dma(2), dma(5), dma(2), dma(5), dma(3), dma(3),
           dma(1), dma(1), dma(2), dma(1), dma(1)]
    )
    in_hbm = lambda a: pltpu.with_memory_space_constraint(a, pltpu.HBM)
    values, grads = pl.pallas_call(
        functools.partial(kernel, (groups, tps, pps, parts, cut)),
        out_shape=(
            jax.ShapeDtypeStruct((rows, kvd), BF),
            jax.ShapeDtypeStruct((grows, dvis), BF),
        ),
        in_specs=[pl.BlockSpec(memory_space=pl.ANY)] * 8,
        out_specs=(pl.BlockSpec(memory_space=pltpu.VMEM), pl.BlockSpec(memory_space=pltpu.VMEM)),
        scratch_shapes=scratch,
        compiler_params=pltpu.CompilerParams(
            collective_id=0, has_side_effects=True, vmem_limit_bytes=48 * 1024 * 1024
        ),
    )(
        *map(
            in_hbm,
            (target.reshape(1, img), slot_place.reshape(1, slots), loss_mask, vision, w_proj, w_value, text_embed, cotangent),
        )
    )
    return values[None], grads[None]


def solution(mesh):
    in_specs = (
        P("pp", "grp", None),
        P("pp", "grp", "tp"),
        P("pp", "grp", None),
        P("pp", "grp", None),
        P("pp", "grp"),
        P(None, "tp"),
        P("tp", None),
        P("pp", "grp", None),
    )
    out_specs = (P("pp", ("grp", "tp"), None), P("pp", ("grp", "tp"), None))
    return jax.shard_map(body, mesh=mesh, in_specs=in_specs, out_specs=out_specs, check_vma=False)
```

```python
import functools

import jax
import jax.numpy as jnp
from jax import lax
from jax.experimental import pallas as pl
from jax.experimental.pallas import tpu as pltpu
from jax.sharding import PartitionSpec as P

MESH = pl.DeviceIdType.MESH
BF, F32, I32 = jnp.bfloat16, jnp.float32, jnp.int32


def iota(shape, dim):
    return lax.broadcasted_iota(I32, shape, dim)


def mm(a, b):
    return jnp.dot(a, b, preferred_element_type=F32)


def mm_nt(a, b):
    return lax.dot_general(a, b, (((1,), (1,)), ((), ())), preferred_element_type=F32)


def flag(cond):
    return jnp.where(cond, 1.0, 0.0).astype(F32)


def to_col(row):
    n = row.shape[1]
    return jnp.sum(jnp.where(iota((n, n), 0) == iota((n, n), 1), row, 0), axis=1, keepdims=True)


def collected(ref, sem, n):
    pltpu.make_async_copy(ref.at[pl.ds(0, n)], ref.at[pl.ds(0, n)], sem).wait()


class Reduce:
    def __init__(self, env, half, pf, pb, pr, sb, r1, fdn, fup, send, recv):
        self.env, self.half = env, half
        self.pf, self.pb, self.pr, self.sb = pf, pb, pr, sb
        self.mine = pf.at[env["core"]]
        h_up, h_dn, h_op = env["h_up"], env["h_dn"], env["h_op"]
        own = lambda h, s: half(sb.at[h], s)
        table = [
            (own(h_op, 0), half(r1, 0), "up"),
            (own(h_op, 1), half(r1, 1), "dn"),
            (own(h_dn, 0), half(fup, 0), "dn"),
            (own(h_up, 1), half(fdn, 1), "up"),
            (own(h_up, 0), half(fdn, 0), "up"),
            (own(h_dn, 1), half(fup, 1), "dn"),
            (half(pb, 0), half(pr, 0), "partner"),
            (half(pb, 1), half(pr, 1), "partner"),
        ]
        self.copies = [
            pltpu.make_async_remote_copy(
                src, dst, send.at[1 if i > 5 else 0], recv.at[i if i < 2 else 2 if i < 6 else i - 3],
                device_id={"tp": env[way]}, device_id_type=MESH,
            )
            for i, (src, dst, way) in enumerate(table)
        ]
        self.r1, self.fdn, self.fup, self.send, self.recv = r1, fdn, fup, send, recv

    def start_pair(self, s):
        half = self.half
        half(self.pb, s)[...] = half(self.pf.at[1 - self.env["core"]], s)[...].astype(BF)
        self.copies[6 + s].start()

    def pair_sum(self, h, s):
        half = self.half
        return half(self.mine.at[h], s)[...] + half(self.pr.at[h], s)[...].astype(F32)

    def first(self, s):
        h = self.env["h_op"]
        self.copies[6 + s].wait_recv()
        self.half(self.sb.at[h], s)[...] = self.pair_sum(h, s).astype(BF)
        self.copies[s].start()

    def direct(self, s):
        h = self.env["h_dn" if s == 0 else "h_up"]
        self.half(self.sb.at[h], s)[...] = self.pair_sum(h, s).astype(BF)
        self.copies[2 + s].start()

    def relay(self, s):
        h = self.env["h_up" if s == 0 else "h_dn"]
        v = self.pair_sum(h, s)
        self.copies[s].wait_recv()
        self.half(self.sb.at[h], s)[...] = (v + self.half(self.r1, s)[...].astype(F32)).astype(BF)
        self.copies[4 + s].start()

    def end(self):
        env = self.env
        collected(self.pr, self.recv.at[2], 2)
        return (
            self.mine[env["hi"]]
            + self.pr[env["hi"]].astype(F32)
            + self.fdn[...].astype(F32)
            + self.fup[...].astype(F32)
        )

    def drain(self):
        collected(self.pb, self.send.at[1], self.pb.shape[0])
        collected(self.sb, self.send.at[0], 3)


def kernel(
    sizes, target, place, loss, vision, w_proj, w_value, text, cot, values_out, grad_out,
    target_v, place_v, loss_v, vision_v, wp_v, wv_v, text_v, cot_v,
    emb_acc, tpf, tpb, tpr, tsb, tr1, tfd, tfu,
    ipf, ipb, ipr, isb, ir1, ifd, ifu,
    gpf, gpb, gpr, gsb, gr1, gfd, gfu,
    xcot, rcot, xmeta, rmeta, ximg, rimg, chalf, zs, zr, tot_s, tot_r,
    load_sem, t_send, t_recv, i_send, i_recv, g_send, g_recv, a_send, a_recv, z_send, z_recv, s_sem, p_send, p_recv,
):
    groups, tps, pps, parts, cut = sizes
    grp, tp, pp = lax.axis_index("grp"), lax.axis_index("tp"), lax.axis_index("pp")
    core, hi = lax.rem(tp, 2), tp // 2
    chips = tps // 2
    env = dict(
        core=core, hi=hi, partner=tp + 1 - 2 * core,
        up=lax.rem(tp + 2, tps), dn=lax.rem(tp + tps - 2, tps),
        h_up=lax.rem(hi + 1, chips), h_dn=lax.rem(hi + chips - 1, chips), h_op=lax.rem(hi + 2, chips),
    )
    img, width = vision_v.shape[0], wp_v.shape[1]
    dvis, seq, kvd = wp_v.shape[0], text_v.shape[0], wv_v.shape[1]
    half_kv = kvd // 2
    slots = place_v.shape[1]
    cap = slots // groups
    kchunk = dvis // parts

    gx, gy = 4, groups // 4
    offsets = [(dx, dy) for dx in range(gx) for dy in range(gy) if dx or dy]
    offsets.sort(key=lambda o: -(min(o[0], gx - o[0]) + min(o[1], gy - o[1])))
    px, py = grp // gy, lax.rem(grp, gy)
    peers = [lax.rem(px + dx, gx) * gy + lax.rem(py + dy, gy) for dx, dy in offsets]

    pairs = [
        (place, place_v), (target, target_v), (loss, loss_v),
        (cot.at[0, :, pl.ds(pl.multiple_of(core * half_kv, 128), half_kv)], cot_v), (vision.at[0], vision_v),
    ] + [(w_proj.at[pl.ds(i * kchunk, kchunk)], wp_v.at[pl.ds(i * kchunk, kchunk)]) for i in range(parts)]
    pairs += [(w_value, wv_v), (text.at[0], text_v)]
    loads = [pltpu.make_async_copy(s, d, load_sem.at[i]) for i, (s, d) in enumerate(pairs)]
    for c in loads[:-2]:
        c.start()
    l_cot, l_vision, l_proj, l_value, l_text = loads[3], loads[4], loads[5:-2], loads[-2], loads[-1]
    barrier = pltpu.get_barrier_semaphore()
    for p in peers:
        pl.semaphore_signal(barrier, inc=1, device_id={"grp": p}, device_id_type=MESH)
    for c in loads[-2:]:
        c.start()
    for i in range(1, tps):
        pl.semaphore_signal(barrier, inc=1, device_id={"tp": lax.rem(tp + i, tps)}, device_id_type=MESH)
    for i in range(1, pps):
        pl.semaphore_signal(barrier, inc=1, device_id={"pp": lax.rem(pp + i, pps)}, device_id_type=MESH)

    for c in loads[:3]:
        c.wait()
    t_row = target_v[...]
    t_col = to_col(t_row)
    same = t_col == t_row
    k_col = jnp.sum(jnp.where(same & (iota((img, img), 1) < iota((img, img), 0)), 1, 0), axis=1, keepdims=True)
    k_row = jnp.sum(jnp.where(same & (iota((img, img), 0) < iota((img, img), 1)), 1, 0), axis=0, keepdims=True)
    counts = jnp.sum(flag(t_col == iota((img, 128), 1)), axis=0, keepdims=True)
    sp_row = place_v[...]
    sp_col = to_col(sp_row)
    loss_f = loss_v[...].astype(F32)
    at_slot = flag(sp_col == iota((slots, seq), 1))
    mask_slot = jnp.sum(at_slot * loss_f, axis=1, keepdims=True)
    eye = iota((slots, slots), 0) == iota((slots, slots), 1)
    mask_row = jnp.sum(jnp.where(eye, mask_slot, 0.0), axis=0, keepdims=True)
    mask_sum = jnp.sum(loss_f, axis=1, keepdims=True)
    r8 = iota((8, 128), 0)
    meta = jnp.where(r8 == 0, counts, jnp.where(r8 == 1, mask_row, jnp.where(r8 == 2, mask_sum, 0.0)))
    xmeta[...] = meta

    d_i = iota((4 * slots, 1), 0)
    d_from = slots * ((d_i // 4) % 4) + 4 * (d_i // 16) + d_i % 4
    shuffle = flag(iota((4 * slots, 4 * slots), 1) == d_from).astype(BF)
    l_cot.wait()
    y = mm(at_slot.astype(BF), cot_v[...]).astype(BF)
    ystack = jnp.concatenate([y[:, 128 * j : 128 * (j + 1)] for j in range(4)], axis=0)
    xcot[...] = mm(shuffle, ystack).astype(BF).reshape(groups, 16, 128)

    l_vision.wait()
    for i in range(parts):
        l_proj[i].wait()
        part = mm(vision_v[:, i * kchunk : (i + 1) * kchunk], wp_v[i * kchunk : (i + 1) * kchunk, :])
        if i == 0:
            emb_acc[...] = part
        else:
            emb_acc[...] += part
    l_value.wait()
    emb = emb_acc[...].astype(BF)
    for t in range(tps):
        if t % 2 == 0:
            res = mm(emb, wv_v[:, 128 * t : 128 * t + 256])
        piece = res[:, 128 * (t % 2) : 128 * (t % 2) + 128]
        for s in range(2):
            ipf[t % 2, t // 2, s] = piece[s * (img // 2) : (s + 1) * (img // 2)]

    lead = lambda ref, s: ref.at[..., s, :, :] if len(ref.shape) == 4 else ref.at[s]
    span = (pl.ds(0, cut), pl.ds(cut, dvis - cut))
    lane_cut = lambda ref, s: ref.at[..., span[s]]
    red_i = Reduce(env, lead, ipf, ipb, ipr, isb, ir1, ifd, ifu, i_send, i_recv)
    red_t = Reduce(env, lead, tpf, tpb, tpr, tsb, tr1, tfd, tfu, t_send, t_recv)
    red_g = Reduce(env, lane_cut, gpf, gpb, gpr, gsb, gr1, gfd, gfu, g_send, g_recv)

    pl.semaphore_wait(barrier, (tps - 1) + (groups - 1) + (pps - 1))

    red_i.start_pair(0)
    red_i.start_pair(1)

    def spread(src, dst, k, whole):
        for p in peers:
            pltpu.make_async_remote_copy(
                src if whole else src.at[p], dst.at[grp], a_send.at[k], a_recv.at[k],
                device_id={"grp": p}, device_id_type=MESH,
            ).start()

    spread(xcot, rcot, 0, False)

    l_text.wait()
    rows_out = seq // tps
    hr = rows_out // 2

    def text_part(n):
        cols = pl.ds(n * 256, 256)
        res = mm(text_v[...], wv_v[:, cols])
        for t in range(tps):
            for s in range(2):
                r0 = t * rows_out + s * hr
                tpf[t % 2, t // 2, s, :, cols] = res[r0 : r0 + hr]

    text_part(0)
    text_part(1)

    red_i.first(0)
    red_i.first(1)
    red_i.direct(0)
    red_i.direct(1)
    for n in range(2, kvd // 256):
        text_part(n)
    red_t.start_pair(0)
    red_t.start_pair(1)
    spread(xmeta, rmeta, 1, True)
    red_t.first(0)
    red_t.first(1)
    red_i.relay(0)
    red_i.relay(1)
    red_t.direct(0)
    red_t.direct(1)

    lane = iota((img, 4 * slots), 1)
    pick = jnp.concatenate(
        [flag(lane == 16 * t_col + 4 * j + k_col).astype(BF) for j in range(4)], axis=0
    )
    collected(rcot, a_recv.at[0], groups - 1)
    rcot[pl.ds(grp, 1)] = xcot[pl.ds(grp, 1)]
    got = mm(pick, rcot[...].reshape(4 * slots, 128)).astype(BF)
    mine = jnp.concatenate([got[img * j : img * (j + 1)] for j in range(4)], axis=1)
    chalf[pl.ds(core, 1)] = mine[None]
    swap = pltpu.make_async_remote_copy(
        chalf.at[core], chalf.at[core], s_sem.at[0], s_sem.at[1], device_id={"tp": env["partner"]}, device_id_type=MESH
    )
    swap.start()

    half_cols = lambda c: pl.ds(pl.multiple_of(c * half_kv, 128), half_kv)
    for n in range(0, width, 256):
        emb_acc[:, n : n + 256] = mm_nt(mine, wv_v[n : n + 256, half_cols(core)])
    swap.wait_recv()
    red_t.relay(0)
    red_t.relay(1)
    other = chalf[1 - core]
    for n in range(0, width, 256):
        emb_acc[:, n : n + 256] += mm_nt(other, wv_v[n : n + 256, half_cols(1 - core)])
    d_img = emb_acc[...].astype(BF)

    def grad_part(lo, up):
        res = mm_nt(d_img, wp_v[lo:up, :])
        for t in range(tps):
            gpf[t % 2, t // 2, :, lo:up] = res[8 * t : 8 * t + 8]

    first = cut // 256 * 128
    grad_part(0, first)

    vals = red_i.end().reshape(img, 128).astype(BF)
    r_slot = flag(iota((8 * groups, img), 0) == 8 * t_row + k_row).astype(BF)
    ximg[...] = mm(r_slot, vals).reshape(groups, 8, 128).astype(BF)
    spread(ximg, rimg, 2, False)
    grad_part(first, cut)
    red_g.start_pair(0)

    mid = cut + (dvis - cut) // 256 * 128
    grad_part(cut, mid)
    red_g.first(0)
    grad_part(mid, dvis)
    red_g.start_pair(1)

    collected(rmeta, a_recv.at[1], groups - 1)
    rmeta[pl.ds(grp, 1)] = xmeta[...][None]
    metas = rmeta[...].reshape(8 * groups, 128).astype(BF)
    e_i, e_l = iota((groups, 8 * groups), 0), iota((groups, 8 * groups), 1)
    c_mat = mm(flag(e_l == 8 * e_i).astype(BF), metas)
    m_mat = mm(flag(e_l == 8 * e_i + 1).astype(BF), metas)
    s_mat = mm(flag(e_l == 8 * e_i + 2).astype(BF), metas)
    fan = flag(iota((groups, slots), 1) // cap == iota((groups, slots), 0)).astype(BF)
    used = lax.dot_general(
        c_mat.astype(BF), fan, (((0,), (0,)), ((), ())), preferred_element_type=F32
    )[:groups]
    k_of = (iota((groups, slots), 1) % cap).astype(F32)
    lost = jnp.sum(jnp.where(k_of < used, m_mat, 0.0)).reshape(1, 1)
    total = jnp.sum(s_mat[:, 0:1]).reshape(1, 1) - lost
    tot_s[...] = jnp.broadcast_to(total, (8, 128))
    tot_copies = []
    for i in range(1, pps):
        tot_copies.append(
            pltpu.make_async_remote_copy(
                tot_s, tot_r.at[i - 1], p_send.at[0], p_recv.at[0],
                device_id={"pp": lax.rem(pp + i, pps)}, device_id_type=MESH,
            )
        )
    red_g.first(1)
    for c in tot_copies:
        c.start()
    red_g.direct(0)
    red_g.direct(1)

    x_l, x_i = iota((slots, 8 * groups), 1), iota((slots, 8 * groups), 0)
    holds = (x_i == cap * (x_l // 8) + x_l % 8) & (x_l % 8 < cap)
    sp8 = jnp.sum(jnp.where(holds, sp_col + 1, 0), axis=0, keepdims=True) - 1
    c_me = jnp.sum(jnp.where(iota((groups, 128), 1) == grp, c_mat, 0.0), axis=1, keepdims=True)
    c8 = jnp.sum(jnp.where(e_l // 8 == e_i, c_me, 0.0), axis=0, keepdims=True)
    valid = (iota((1, 8 * groups), 1) % 8).astype(F32) < c8
    pos8 = jnp.where(valid, sp8, -1)
    put = flag(iota((seq, 8 * groups), 0) == pos8).astype(BF)
    collected(rimg, a_recv.at[2], groups - 1)
    rimg[pl.ds(grp, 1)] = ximg[pl.ds(grp, 1)]
    zs[...] = mm(put, rimg[...].astype(F32).reshape(8 * groups, 128).astype(BF)).astype(BF).reshape(tps, rows_out, 128)
    z_copies = []
    for i in (4, 3, 5, 2, 6, 1, 7):
        peer = lax.rem(tp + i, tps)
        z_copies.append(
            pltpu.make_async_remote_copy(
                zs.at[peer], zr.at[tp], z_send.at[0], z_recv.at[0], device_id={"tp": peer}, device_id_type=MESH
            )
        )
        z_copies[-1].start()

    red_g.relay(0)
    red_g.relay(1)
    text_vals = red_t.end().reshape(rows_out, kvd)
    is_img = jnp.sum(flag(iota((rows_out, 8 * groups), 0) + rows_out * tp == pos8), axis=1, keepdims=True)
    collected(zr, z_recv.at[0], tps - 1)
    zr[pl.ds(tp, 1)] = zs[pl.ds(tp, 1)]
    for t in range(tps):
        cols = slice(128 * t, 128 * t + 128)
        values_out[:, cols] = jnp.where(is_img > 0.5, zr[t].astype(F32), text_vals[:, cols]).astype(BF)

    collected(tot_r, p_recv.at[0], pps - 1)
    text_total = tot_s[...]
    for i in range(1, pps):
        text_total = text_total + tot_r[i - 1]
    scale = (jnp.full((8, 128), float(pps * groups * seq), F32) / text_total)[:, 0:1]
    grad_out[...] = (red_g.end() * scale).astype(BF)

    for r in (red_i, red_t, red_g):
        r.drain()
    collected(xcot, a_send.at[0], groups - 1)
    collected(rmeta, a_send.at[1], groups - 1)
    collected(ximg, a_send.at[2], groups - 1)
    swap.wait_send()
    collected(zs, z_send.at[0], tps - 1)
    collected(tot_r, p_send.at[0], pps - 1)


def put_out(values, grads, values_out, grads_out, sems):
    copies = [
        pltpu.make_async_copy(values, values_out.at[0], sems.at[0]),
        pltpu.make_async_copy(grads, grads_out.at[0], sems.at[1]),
    ]
    for c in copies:
        c.start()
    for c in copies:
        c.wait()


def body(vision, text_embed, target, slot_place, loss_mask, w_proj, w_value, cotangent):
    groups, tps, pps = lax.axis_size("grp"), lax.axis_size("tp"), lax.axis_size("pp")
    img, dvis, width = vision.shape[1], vision.shape[2], w_proj.shape[1]
    seq, kvd, slots = text_embed.shape[1], w_value.shape[1], slot_place.shape[2]
    chips, parts = tps // 2, 5
    cut = dvis * 3 // 5 // 128 * 128
    rows, grows = seq // tps, img // tps
    vm = pltpu.VMEM
    dma = lambda *s: pltpu.SemaphoreType.DMA(s)

    def reduce_bufs(chunk):
        return [
            vm((2, chips) + chunk, F32), vm((chips,) + chunk, BF), vm((chips,) + chunk, BF), vm((chips,) + chunk, BF),
            vm(chunk, BF), vm(chunk, BF), vm(chunk, BF),
        ]

    scratch = (
        [vm((1, img), I32), vm((1, slots), I32), vm((1, seq), I32), vm((img, dvis), BF), vm((dvis, width), BF),
         vm((width, kvd), BF), vm((seq, width), BF), vm((seq, kvd // 2), BF), vm((img, width), F32)]
        + reduce_bufs((2, rows // 2, kvd))
        + reduce_bufs((2, img // 2, 128))
        + reduce_bufs((grows, dvis))
        + [vm((groups, 16, 128), BF), vm((groups, 16, 128), BF), vm((8, 128), F32), vm((groups, 8, 128), F32),
           vm((groups, 8, 128), BF), vm((groups, 8, 128), BF), vm((2, img, kvd // 2), BF),
           vm((tps, rows, 128), BF), vm((tps, rows, 128), BF), vm((8, 128), F32), vm((pps - 1, 8, 128), F32)]
        + [dma(7 + parts), dma(2), dma(5), dma(2), dma(5), dma(2), dma(5), dma(3), dma(3),
           dma(1), dma(1), dma(2), dma(1), dma(1)]
    )
    in_hbm = lambda a: pltpu.with_memory_space_constraint(a, pltpu.HBM)
    values, grads = pl.pallas_call(
        functools.partial(kernel, (groups, tps, pps, parts, cut)),
        out_shape=(
            jax.ShapeDtypeStruct((rows, kvd), BF),
            jax.ShapeDtypeStruct((grows, dvis), BF),
        ),
        in_specs=[pl.BlockSpec(memory_space=pl.ANY)] * 8,
        out_specs=(pl.BlockSpec(memory_space=pltpu.VMEM), pl.BlockSpec(memory_space=pltpu.VMEM)),
        scratch_shapes=scratch,
        compiler_params=pltpu.CompilerParams(
            collective_id=0, has_side_effects=True, vmem_limit_bytes=48 * 1024 * 1024
        ),
    )(
        *map(
            in_hbm,
            (target.reshape(1, img), slot_place.reshape(1, slots), loss_mask, vision, w_proj, w_value, text_embed, cotangent),
        )
    )
    return pl.pallas_call(
        put_out,
        out_shape=(jax.ShapeDtypeStruct((1, rows, kvd), BF), jax.ShapeDtypeStruct((1, grows, dvis), BF)),
        in_specs=[pl.BlockSpec(memory_space=pltpu.VMEM)] * 2,
        out_specs=(pl.BlockSpec(memory_space=pltpu.HBM), pl.BlockSpec(memory_space=pltpu.HBM)),
        scratch_shapes=[dma(2)],
        compiler_params=pltpu.CompilerParams(vmem_limit_bytes=4 * 1024 * 1024),
    )(values, grads)


def solution(mesh):
    in_specs = (
        P("pp", "grp", None),
        P("pp", "grp", "tp"),
        P("pp", "grp", None),
        P("pp", "grp", None),
        P("pp", "grp"),
        P(None, "tp"),
        P("tp", None),
        P("pp", "grp", None),
    )
    out_specs = (P("pp", ("grp", "tp"), None), P("pp", ("grp", "tp"), None))
    return jax.shard_map(body, mesh=mesh, in_specs=in_specs, out_specs=out_specs, check_vma=False)
```

```python
import functools

import jax
import jax.numpy as jnp
from jax import lax
from jax.experimental import pallas as pl
from jax.experimental.pallas import tpu as pltpu
from jax.sharding import PartitionSpec as P

MESH = pl.DeviceIdType.MESH
BF, F32, I32 = jnp.bfloat16, jnp.float32, jnp.int32


def iota(shape, dim):
    return lax.broadcasted_iota(I32, shape, dim)


def mm(a, b):
    return jnp.dot(a, b, preferred_element_type=F32)


def mm_nt(a, b):
    return lax.dot_general(a, b, (((1,), (1,)), ((), ())), preferred_element_type=F32)


def flag(cond):
    return jnp.where(cond, 1.0, 0.0).astype(F32)


def to_col(row):
    n = row.shape[1]
    return jnp.sum(jnp.where(iota((n, n), 0) == iota((n, n), 1), row, 0), axis=1, keepdims=True)


def collected(ref, sem, n):
    pltpu.make_async_copy(ref.at[pl.ds(0, n)], ref.at[pl.ds(0, n)], sem).wait()


class Reduce:
    def __init__(self, env, half, pieces, pf, pb, pr, sb, r1, fdn, fup, send, recv):
        self.env, self.half, self.pieces = env, half, pieces
        self.pf, self.pb, self.pr, self.sb = pf, pb, pr, sb
        self.mine = pf.at[env["core"]]
        h_up, h_dn, h_op = env["h_up"], env["h_dn"], env["h_op"]
        own = lambda h, s: half(sb.at[h], s)
        n = len(pieces[0])

        def copy(src, dst, way, out, got):
            return pltpu.make_async_remote_copy(
                src, dst, send.at[out], recv.at[got], device_id={"tp": env[way]}, device_id_type=MESH
            )

        ways = (("up", h_up, fdn), ("dn", h_dn, fup))
        self.pair = [copy(half(pb, s), half(pr, s), "partner", 1, s) for s in range(2)]
        self.firsts = [
            [copy(p(sb.at[h_op]), p(r1), ways[s][0], 0, 3 + s * n + u) for u, p in enumerate(pieces[s])]
            for s in range(2)
        ]
        self.directs = [
            copy(own(ways[1 - s][1], s), half(ways[1 - s][2], s), ways[1 - s][0], 0, 2) for s in range(2)
        ]
        self.relays = [
            [copy(p(sb.at[ways[s][1]]), p(ways[s][2]), ways[s][0], 0, 2) for p in pieces[s]] for s in range(2)
        ]
        self.r1, self.fdn, self.fup, self.send, self.recv = r1, fdn, fup, send, recv

    def start_pair(self, s):
        half = self.half
        half(self.pb, s)[...] = half(self.pf.at[1 - self.env["core"]], s)[...].astype(BF)
        self.pair[s].start()

    def pair_sum(self, h, s):
        half = self.half
        return half(self.mine.at[h], s)[...] + half(self.pr.at[h], s)[...].astype(F32)

    def first(self, s):
        h = self.env["h_op"]
        self.pair[s].wait_recv()
        self.half(self.sb.at[h], s)[...] = self.pair_sum(h, s).astype(BF)
        for c in self.firsts[s]:
            c.start()

    def direct(self, s):
        h = self.env["h_dn" if s == 0 else "h_up"]
        self.half(self.sb.at[h], s)[...] = self.pair_sum(h, s).astype(BF)
        self.directs[s].start()

    def relay(self, s):
        h = self.env["h_up" if s == 0 else "h_dn"]
        for p, got, out in zip(self.pieces[s], self.firsts[s], self.relays[s]):
            v = p(self.mine.at[h])[...] + p(self.pr.at[h])[...].astype(F32)
            got.wait_recv()
            p(self.sb.at[h])[...] = (v + p(self.r1)[...].astype(F32)).astype(BF)
            out.start()

    def end(self):
        env = self.env
        collected(self.pr, self.recv.at[2], 2)
        return (
            self.mine[env["hi"]]
            + self.pr[env["hi"]].astype(F32)
            + self.fdn[...].astype(F32)
            + self.fup[...].astype(F32)
        )

    def drain(self):
        collected(self.pb, self.send.at[1], self.pb.shape[0])
        collected(self.sb, self.send.at[0], 3)


def kernel(
    sizes, target, place, loss, vision, w_proj, w_value, text, cot, values_out, grad_out,
    target_v, place_v, loss_v, vision_v, wp_v, wv_v, text_v, cot_v,
    emb_acc, tpf, tpb, tpr, tsb, tr1, tfd, tfu,
    ipf, ipb, ipr, isb, ir1, ifd, ifu,
    gpf, gpb, gpr, gsb, gr1, gfd, gfu,
    xcot, rcot, xmeta, rmeta, ximg, rimg, chalf, zs, zr, tot_s, tot_r,
    load_sem, t_send, t_recv, i_send, i_recv, g_send, g_recv, a_send, a_recv, z_send, z_recv, s_sem, p_send, p_recv,
):
    groups, tps, pps, parts, cut = sizes
    grp, tp, pp = lax.axis_index("grp"), lax.axis_index("tp"), lax.axis_index("pp")
    core, hi = lax.rem(tp, 2), tp // 2
    chips = tps // 2
    env = dict(
        core=core, hi=hi, partner=tp + 1 - 2 * core,
        up=lax.rem(tp + 2, tps), dn=lax.rem(tp + tps - 2, tps),
        h_up=lax.rem(hi + 1, chips), h_dn=lax.rem(hi + chips - 1, chips), h_op=lax.rem(hi + 2, chips),
    )
    img, width = vision_v.shape[0], wp_v.shape[1]
    dvis, seq, kvd = wp_v.shape[0], text_v.shape[0], wv_v.shape[1]
    half_kv = kvd // 2
    slots = place_v.shape[1]
    cap = slots // groups
    kchunk = dvis // parts

    gx, gy = 4, groups // 4
    offsets = [(dx, dy) for dx in range(gx) for dy in range(gy) if dx or dy]
    offsets.sort(key=lambda o: -(min(o[0], gx - o[0]) + min(o[1], gy - o[1])))
    px, py = grp // gy, lax.rem(grp, gy)
    peers = [lax.rem(px + dx, gx) * gy + lax.rem(py + dy, gy) for dx, dy in offsets]

    pairs = [
        (place, place_v), (target, target_v), (loss, loss_v),
        (cot.at[0, :, pl.ds(pl.multiple_of(core * half_kv, 128), half_kv)], cot_v), (vision.at[0], vision_v),
    ] + [(w_proj.at[pl.ds(i * kchunk, kchunk)], wp_v.at[pl.ds(i * kchunk, kchunk)]) for i in range(parts)]
    pairs += [(w_value, wv_v), (text.at[0], text_v)]
    loads = [pltpu.make_async_copy(s, d, load_sem.at[i]) for i, (s, d) in enumerate(pairs)]
    for c in loads[:-2]:
        c.start()
    l_cot, l_vision, l_proj, l_value, l_text = loads[3], loads[4], loads[5:-2], loads[-2], loads[-1]
    barrier = pltpu.get_barrier_semaphore()
    for p in peers:
        pl.semaphore_signal(barrier, inc=1, device_id={"grp": p}, device_id_type=MESH)
    for c in loads[-2:]:
        c.start()
    for i in range(1, tps):
        pl.semaphore_signal(barrier, inc=1, device_id={"tp": lax.rem(tp + i, tps)}, device_id_type=MESH)
    for i in range(1, pps):
        pl.semaphore_signal(barrier, inc=1, device_id={"pp": lax.rem(pp + i, pps)}, device_id_type=MESH)

    for c in loads[:3]:
        c.wait()
    t_row = target_v[...]
    t_col = to_col(t_row)
    same = t_col == t_row
    k_col = jnp.sum(jnp.where(same & (iota((img, img), 1) < iota((img, img), 0)), 1, 0), axis=1, keepdims=True)
    k_row = jnp.sum(jnp.where(same & (iota((img, img), 0) < iota((img, img), 1)), 1, 0), axis=0, keepdims=True)
    counts = jnp.sum(flag(t_col == iota((img, 128), 1)), axis=0, keepdims=True)
    sp_row = place_v[...]
    sp_col = to_col(sp_row)
    loss_f = loss_v[...].astype(F32)
    at_slot = flag(sp_col == iota((slots, seq), 1))
    mask_slot = jnp.sum(at_slot * loss_f, axis=1, keepdims=True)
    eye = iota((slots, slots), 0) == iota((slots, slots), 1)
    mask_row = jnp.sum(jnp.where(eye, mask_slot, 0.0), axis=0, keepdims=True)
    mask_sum = jnp.sum(loss_f, axis=1, keepdims=True)
    r8 = iota((8, 128), 0)
    meta = jnp.where(r8 == 0, counts, jnp.where(r8 == 1, mask_row, jnp.where(r8 == 2, mask_sum, 0.0)))
    xmeta[...] = meta.astype(BF)

    d_i = iota((4 * slots, 1), 0)
    d_from = slots * ((d_i // 4) % 4) + 4 * (d_i // 16) + d_i % 4
    shuffle = flag(iota((4 * slots, 4 * slots), 1) == d_from).astype(BF)
    l_cot.wait()
    y = mm(at_slot.astype(BF), cot_v[...]).astype(BF)
    ystack = jnp.concatenate([y[:, 128 * j : 128 * (j + 1)] for j in range(4)], axis=0)
    xcot[...] = mm(shuffle, ystack).astype(BF).reshape(groups, 16, 128)

    l_vision.wait()
    for i in range(parts):
        l_proj[i].wait()
        part = mm(vision_v[:, i * kchunk : (i + 1) * kchunk], wp_v[i * kchunk : (i + 1) * kchunk, :])
        if i == 0:
            emb_acc[...] = part
        else:
            emb_acc[...] += part
    l_value.wait()
    emb = emb_acc[...].astype(BF)
    for t in range(tps):
        if t % 2 == 0:
            res = mm(emb, wv_v[:, 128 * t : 128 * t + 256])
        piece = res[:, 128 * (t % 2) : 128 * (t % 2) + 128]
        for s in range(2):
            ipf[t % 2, t // 2, s] = piece[s * (img // 2) : (s + 1) * (img // 2)]

    lead = lambda ref, s: ref.at[..., s, :, :] if len(ref.shape) == 4 else ref.at[s]
    span = (pl.ds(0, cut), pl.ds(cut, dvis - cut))
    lane_cut = lambda ref, s: ref.at[..., span[s]]
    whole = [[lambda ref, s=s: lead(ref, s)] for s in range(2)]
    mids = ((0, cut // 256 * 128, cut), (cut, cut + (dvis - cut) // 256 * 128, dvis))
    parts_g = [[lambda ref, lo=lo, up=up: ref.at[..., pl.ds(lo, up - lo)] for lo, up in zip(m[:-1], m[1:])] for m in mids]
    red_i = Reduce(env, lead, whole, ipf, ipb, ipr, isb, ir1, ifd, ifu, i_send, i_recv)
    red_t = Reduce(env, lead, whole, tpf, tpb, tpr, tsb, tr1, tfd, tfu, t_send, t_recv)
    red_g = Reduce(env, lane_cut, parts_g, gpf, gpb, gpr, gsb, gr1, gfd, gfu, g_send, g_recv)

    pl.semaphore_wait(barrier, (tps - 1) + (groups - 1) + (pps - 1))

    red_i.start_pair(0)
    red_i.start_pair(1)

    def spread(src, dst, k, whole):
        for p in peers:
            pltpu.make_async_remote_copy(
                src if whole else src.at[p], dst.at[grp], a_send.at[k], a_recv.at[k],
                device_id={"grp": p}, device_id_type=MESH,
            ).start()

    spread(xcot, rcot, 0, False)

    l_text.wait()
    rows_out = seq // tps
    hr = rows_out // 2

    def text_part(n):
        cols = pl.ds(n * 256, 256)
        res = mm(text_v[...], wv_v[:, cols])
        for t in range(tps):
            for s in range(2):
                r0 = t * rows_out + s * hr
                tpf[t % 2, t // 2, s, :, cols] = res[r0 : r0 + hr]

    text_part(0)
    text_part(1)

    red_i.first(0)
    red_i.first(1)
    red_i.direct(0)
    red_i.direct(1)
    for n in range(2, kvd // 256):
        text_part(n)
    red_t.start_pair(0)
    red_t.start_pair(1)
    red_t.first(0)
    red_t.first(1)
    red_i.relay(0)
    red_i.relay(1)
    red_t.direct(0)
    red_t.direct(1)

    lane = iota((img, 4 * slots), 1)
    pick = jnp.concatenate(
        [flag(lane == 16 * t_col + 4 * j + k_col).astype(BF) for j in range(4)], axis=0
    )
    collected(rcot, a_recv.at[0], groups - 1)
    rcot[pl.ds(grp, 1)] = xcot[pl.ds(grp, 1)]
    got = mm(pick, rcot[...].reshape(4 * slots, 128)).astype(BF)
    mine = jnp.concatenate([got[img * j : img * (j + 1)] for j in range(4)], axis=1)
    chalf[pl.ds(core, 1)] = mine[None]
    swap = pltpu.make_async_remote_copy(
        chalf.at[core], chalf.at[core], s_sem.at[0], s_sem.at[1], device_id={"tp": env["partner"]}, device_id_type=MESH
    )
    swap.start()

    spread(xmeta, rmeta, 1, True)

    half_cols = lambda c: pl.ds(pl.multiple_of(c * half_kv, 128), half_kv)
    for n in range(0, width, 256):
        emb_acc[:, n : n + 256] = mm_nt(mine, wv_v[n : n + 256, half_cols(core)])
    swap.wait_recv()
    red_t.relay(0)
    red_t.relay(1)
    other = chalf[1 - core]
    for n in range(0, width, 256):
        emb_acc[:, n : n + 256] += mm_nt(other, wv_v[n : n + 256, half_cols(1 - core)])
    d_img = emb_acc[...].astype(BF)

    def grad_part(lo, up):
        res = mm_nt(d_img, wp_v[lo:up, :])
        for t in range(tps):
            gpf[t % 2, t // 2, :, lo:up] = res[8 * t : 8 * t + 8]

    first = cut // 256 * 128
    grad_part(0, first)

    r_slot = flag(iota((8 * groups, img), 0) == 8 * t_row + k_row).astype(BF)
    vals = red_i.end().reshape(img, 128).astype(BF)
    ximg[...] = mm(r_slot, vals).reshape(groups, 8, 128).astype(BF)
    spread(ximg, rimg, 2, False)
    grad_part(first, cut)
    red_g.start_pair(0)

    mid = cut + (dvis - cut) // 256 * 128
    grad_part(cut, mid)
    red_g.first(0)
    grad_part(mid, dvis)
    red_g.start_pair(1)

    red_g.first(1)
    red_g.direct(1)

    collected(rmeta, a_recv.at[1], groups - 1)
    rmeta[pl.ds(grp, 1)] = xmeta[...][None]
    metas = rmeta[...].astype(F32).reshape(8 * groups, 128).astype(BF)
    e_i, e_l = iota((groups, 8 * groups), 0), iota((groups, 8 * groups), 1)
    c_mat = mm(flag(e_l == 8 * e_i).astype(BF), metas)
    m_mat = mm(flag(e_l == 8 * e_i + 1).astype(BF), metas)
    s_mat = mm(flag(e_l == 8 * e_i + 2).astype(BF), metas)
    fan = flag(iota((groups, slots), 1) // cap == iota((groups, slots), 0)).astype(BF)
    used = lax.dot_general(
        c_mat.astype(BF), fan, (((0,), (0,)), ((), ())), preferred_element_type=F32
    )[:groups]
    k_of = (iota((groups, slots), 1) % cap).astype(F32)
    lost = jnp.sum(jnp.where(k_of < used, m_mat, 0.0)).reshape(1, 1)
    total = jnp.sum(s_mat[:, 0:1]).reshape(1, 1) - lost
    tot_s[...] = jnp.broadcast_to(total, (8, 128))
    tot_copies = []
    for i in range(1, pps):
        tot_copies.append(
            pltpu.make_async_remote_copy(
                tot_s, tot_r.at[i - 1], p_send.at[0], p_recv.at[0],
                device_id={"pp": lax.rem(pp + i, pps)}, device_id_type=MESH,
            )
        )
    for c in tot_copies:
        c.start()

    x_l, x_i = iota((slots, 8 * groups), 1), iota((slots, 8 * groups), 0)
    holds = (x_i == cap * (x_l // 8) + x_l % 8) & (x_l % 8 < cap)
    sp8 = jnp.sum(jnp.where(holds, sp_col + 1, 0), axis=0, keepdims=True) - 1
    c_me = jnp.sum(jnp.where(iota((groups, 128), 1) == grp, c_mat, 0.0), axis=1, keepdims=True)
    c8 = jnp.sum(jnp.where(e_l // 8 == e_i, c_me, 0.0), axis=0, keepdims=True)
    valid = (iota((1, 8 * groups), 1) % 8).astype(F32) < c8
    pos8 = jnp.where(valid, sp8, -1)
    put = flag(iota((seq, 8 * groups), 0) == pos8).astype(BF)
    collected(rimg, a_recv.at[2], groups - 1)
    rimg[pl.ds(grp, 1)] = ximg[pl.ds(grp, 1)]
    zs[...] = mm(put, rimg[...].astype(F32).reshape(8 * groups, 128).astype(BF)).astype(BF).reshape(tps, rows_out, 128)
    z_copies = []
    for i in (4, 3, 5, 2, 6, 1, 7):
        peer = lax.rem(tp + i, tps)
        z_copies.append(
            pltpu.make_async_remote_copy(
                zs.at[peer], zr.at[tp], z_send.at[0], z_recv.at[0], device_id={"tp": peer}, device_id_type=MESH
            )
        )
        z_copies[-1].start()

    red_g.direct(0)
    red_g.relay(0)
    red_g.relay(1)
    text_vals = red_t.end().reshape(rows_out, kvd)
    is_img = jnp.sum(flag(iota((rows_out, 8 * groups), 0) + rows_out * tp == pos8), axis=1, keepdims=True)
    collected(zr, z_recv.at[0], tps - 1)
    zr[pl.ds(tp, 1)] = zs[pl.ds(tp, 1)]
    for t in range(tps):
        cols = slice(128 * t, 128 * t + 128)
        values_out[:, cols] = jnp.where(is_img > 0.5, zr[t].astype(F32), text_vals[:, cols]).astype(BF)

    collected(tot_r, p_recv.at[0], pps - 1)
    text_total = tot_s[...]
    for i in range(1, pps):
        text_total = text_total + tot_r[i - 1]
    scale = (jnp.full((8, 128), float(pps * groups * seq), F32) / text_total)[:, 0:1]
    grad_out[...] = (red_g.end() * scale).astype(BF)

    for r in (red_i, red_t, red_g):
        r.drain()
    collected(xcot, a_send.at[0], groups - 1)
    collected(rmeta, a_send.at[1], groups - 1)
    collected(ximg, a_send.at[2], groups - 1)
    swap.wait_send()
    collected(zs, z_send.at[0], tps - 1)
    collected(tot_r, p_send.at[0], pps - 1)


def put_out(values, grads, values_out, grads_out, sems):
    copies = [
        pltpu.make_async_copy(values, values_out.at[0], sems.at[0]),
        pltpu.make_async_copy(grads, grads_out.at[0], sems.at[1]),
    ]
    for c in copies:
        c.start()
    for c in copies:
        c.wait()


def body(vision, text_embed, target, slot_place, loss_mask, w_proj, w_value, cotangent):
    groups, tps, pps = lax.axis_size("grp"), lax.axis_size("tp"), lax.axis_size("pp")
    img, dvis, width = vision.shape[1], vision.shape[2], w_proj.shape[1]
    seq, kvd, slots = text_embed.shape[1], w_value.shape[1], slot_place.shape[2]
    chips, parts = tps // 2, 5
    cut = dvis * 3 // 5 // 128 * 128
    rows, grows = seq // tps, img // tps
    vm = pltpu.VMEM
    dma = lambda *s: pltpu.SemaphoreType.DMA(s)

    def reduce_bufs(chunk):
        return [
            vm((2, chips) + chunk, F32), vm((chips,) + chunk, BF), vm((chips,) + chunk, BF), vm((chips,) + chunk, BF),
            vm(chunk, BF), vm(chunk, BF), vm(chunk, BF),
        ]

    scratch = (
        [vm((1, img), I32), vm((1, slots), I32), vm((1, seq), I32), vm((img, dvis), BF), vm((dvis, width), BF),
         vm((width, kvd), BF), vm((seq, width), BF), vm((seq, kvd // 2), BF), vm((img, width), F32)]
        + reduce_bufs((2, rows // 2, kvd))
        + reduce_bufs((2, img // 2, 128))
        + reduce_bufs((grows, dvis))
        + [vm((groups, 16, 128), BF), vm((groups, 16, 128), BF), vm((8, 128), BF), vm((groups, 8, 128), BF),
           vm((groups, 8, 128), BF), vm((groups, 8, 128), BF), vm((2, img, kvd // 2), BF),
           vm((tps, rows, 128), BF), vm((tps, rows, 128), BF), vm((8, 128), F32), vm((pps - 1, 8, 128), F32)]
        + [dma(7 + parts), dma(2), dma(5), dma(2), dma(5), dma(2), dma(7), dma(3), dma(3),
           dma(1), dma(1), dma(2), dma(1), dma(1)]
    )
    in_hbm = lambda a: pltpu.with_memory_space_constraint(a, pltpu.HBM)
    values, grads = pl.pallas_call(
        functools.partial(kernel, (groups, tps, pps, parts, cut)),
        out_shape=(
            jax.ShapeDtypeStruct((rows, kvd), BF),
            jax.ShapeDtypeStruct((grows, dvis), BF),
        ),
        in_specs=[pl.BlockSpec(memory_space=pl.ANY)] * 8,
        out_specs=(pl.BlockSpec(memory_space=pltpu.VMEM), pl.BlockSpec(memory_space=pltpu.VMEM)),
        scratch_shapes=scratch,
        compiler_params=pltpu.CompilerParams(
            collective_id=0, has_side_effects=True, vmem_limit_bytes=48 * 1024 * 1024
        ),
    )(
        *map(
            in_hbm,
            (target.reshape(1, img), slot_place.reshape(1, slots), loss_mask, vision, w_proj, w_value, text_embed, cotangent),
        )
    )
    return pl.pallas_call(
        put_out,
        out_shape=(jax.ShapeDtypeStruct((1, rows, kvd), BF), jax.ShapeDtypeStruct((1, grows, dvis), BF)),
        in_specs=[pl.BlockSpec(memory_space=pltpu.VMEM)] * 2,
        out_specs=(pl.BlockSpec(memory_space=pltpu.HBM), pl.BlockSpec(memory_space=pltpu.HBM)),
        scratch_shapes=[dma(2)],
        compiler_params=pltpu.CompilerParams(vmem_limit_bytes=4 * 1024 * 1024),
    )(values, grads)


def solution(mesh):
    in_specs = (
        P("pp", "grp", None),
        P("pp", "grp", "tp"),
        P("pp", "grp", None),
        P("pp", "grp", None),
        P("pp", "grp"),
        P(None, "tp"),
        P("tp", None),
        P("pp", "grp", None),
    )
    out_specs = (P("pp", ("grp", "tp"), None), P("pp", ("grp", "tp"), None))
    return jax.shard_map(body, mesh=mesh, in_specs=in_specs, out_specs=out_specs, check_vma=False)
```

```python
import functools

import jax
import jax.numpy as jnp
from jax import lax
from jax.experimental import pallas as pl
from jax.experimental.pallas import tpu as pltpu
from jax.sharding import PartitionSpec as P

MESH = pl.DeviceIdType.MESH
BF, F32, I32 = jnp.bfloat16, jnp.float32, jnp.int32


def iota(shape, dim):
    return lax.broadcasted_iota(I32, shape, dim)


def mm(a, b):
    return jnp.dot(a, b, preferred_element_type=F32)


def mm_nt(a, b):
    return lax.dot_general(a, b, (((1,), (1,)), ((), ())), preferred_element_type=F32)


def flag(cond):
    return jnp.where(cond, 1.0, 0.0).astype(F32)


def to_col(row):
    n = row.shape[1]
    return jnp.sum(jnp.where(iota((n, n), 0) == iota((n, n), 1), row, 0), axis=1, keepdims=True)


def collected(ref, sem, n):
    pltpu.make_async_copy(ref.at[pl.ds(0, n)], ref.at[pl.ds(0, n)], sem).wait()


class Reduce:
    def __init__(self, env, half, pieces, pf, pb, pr, sb, r1, fdn, fup, send, recv):
        self.env, self.half, self.pieces = env, half, pieces
        self.pf, self.pb, self.pr, self.sb = pf, pb, pr, sb
        self.mine = pf.at[env["core"]]
        h_up, h_dn, h_op = env["h_up"], env["h_dn"], env["h_op"]
        own = lambda h, s: half(sb.at[h], s)
        n = len(pieces[0])

        def copy(src, dst, way, out, got):
            return pltpu.make_async_remote_copy(
                src, dst, send.at[out], recv.at[got], device_id={"tp": env[way]}, device_id_type=MESH
            )

        ways = (("up", h_up, fdn), ("dn", h_dn, fup))
        self.pair = [copy(half(pb, s), half(pr, s), "partner", 1, s) for s in range(2)]
        self.firsts = [
            [copy(p(sb.at[h_op]), p(r1), ways[s][0], 0, 3 + s * n + u) for u, p in enumerate(pieces[s])]
            for s in range(2)
        ]
        self.directs = [
            copy(own(ways[1 - s][1], s), half(ways[1 - s][2], s), ways[1 - s][0], 0, 2) for s in range(2)
        ]
        self.relays = [
            [copy(p(sb.at[ways[s][1]]), p(ways[s][2]), ways[s][0], 0, 2) for p in pieces[s]] for s in range(2)
        ]
        self.r1, self.fdn, self.fup, self.send, self.recv = r1, fdn, fup, send, recv

    def start_pair(self, s):
        half = self.half
        half(self.pb, s)[...] = half(self.pf.at[1 - self.env["core"]], s)[...].astype(BF)
        self.pair[s].start()

    def pair_sum(self, h, s):
        half = self.half
        return half(self.mine.at[h], s)[...] + half(self.pr.at[h], s)[...].astype(F32)

    def first(self, s):
        h = self.env["h_op"]
        self.pair[s].wait_recv()
        self.half(self.sb.at[h], s)[...] = self.pair_sum(h, s).astype(BF)
        for c in self.firsts[s]:
            c.start()

    def direct(self, s):
        h = self.env["h_dn" if s == 0 else "h_up"]
        self.half(self.sb.at[h], s)[...] = self.pair_sum(h, s).astype(BF)
        self.directs[s].start()

    def relay(self, s):
        h = self.env["h_up" if s == 0 else "h_dn"]
        for p, got, out in zip(self.pieces[s], self.firsts[s], self.relays[s]):
            v = p(self.mine.at[h])[...] + p(self.pr.at[h])[...].astype(F32)
            got.wait_recv()
            p(self.sb.at[h])[...] = (v + p(self.r1)[...].astype(F32)).astype(BF)
            out.start()

    def end(self):
        env = self.env
        collected(self.pr, self.recv.at[2], 2)
        return (
            self.mine[env["hi"]]
            + self.pr[env["hi"]].astype(F32)
            + self.fdn[...].astype(F32)
            + self.fup[...].astype(F32)
        )

    def drain(self):
        collected(self.pb, self.send.at[1], self.pb.shape[0])
        collected(self.sb, self.send.at[0], 3)


def kernel(
    sizes, target, place, loss, vision, w_proj, w_value, text, cot, values_out, grad_out,
    target_v, place_v, loss_v, vision_v, wp_v, wv_v, text_v, cot_v,
    emb_acc, tpf, tpb, tpr, tsb, tr1, tfd, tfu,
    ipf, ipb, ipr, isb, ir1, ifd, ifu,
    gpf, gpb, gpr, gsb, gr1, gfd, gfu,
    xcot, rcot, xmeta, rmeta, ximg, rimg, chalf, zs, zr, tot_s, tot_r,
    load_sem, t_send, t_recv, i_send, i_recv, g_send, g_recv, a_send, a_recv, z_send, z_recv, s_sem, p_send, p_recv,
):
    groups, tps, pps, parts, cut = sizes
    grp, tp, pp = lax.axis_index("grp"), lax.axis_index("tp"), lax.axis_index("pp")
    core, hi = lax.rem(tp, 2), tp // 2
    chips = tps // 2
    env = dict(
        core=core, hi=hi, partner=tp + 1 - 2 * core,
        up=lax.rem(tp + 2, tps), dn=lax.rem(tp + tps - 2, tps),
        h_up=lax.rem(hi + 1, chips), h_dn=lax.rem(hi + chips - 1, chips), h_op=lax.rem(hi + 2, chips),
    )
    img, width = vision_v.shape[0], wp_v.shape[1]
    dvis, seq, kvd = wp_v.shape[0], text_v.shape[0], wv_v.shape[1]
    half_kv = kvd // 2
    slots = place_v.shape[1]
    cap = slots // groups
    kchunk = dvis // parts

    gx, gy = 4, groups // 4
    offsets = [(dx, dy) for dx in range(gx) for dy in range(gy) if dx or dy]
    offsets.sort(key=lambda o: -(min(o[0], gx - o[0]) + min(o[1], gy - o[1])))
    px, py = grp // gy, lax.rem(grp, gy)
    peers = [lax.rem(px + dx, gx) * gy + lax.rem(py + dy, gy) for dx, dy in offsets]

    pairs = [
        (place, place_v), (target, target_v), (loss, loss_v),
        (cot.at[0, :, pl.ds(pl.multiple_of(core * half_kv, 128), half_kv)], cot_v), (vision.at[0], vision_v),
    ] + [(w_proj.at[pl.ds(i * kchunk, kchunk)], wp_v.at[pl.ds(i * kchunk, kchunk)]) for i in range(parts)]
    pairs += [(w_value, wv_v), (text.at[0], text_v)]
    loads = [pltpu.make_async_copy(s, d, load_sem.at[i]) for i, (s, d) in enumerate(pairs)]
    for c in loads[:-2]:
        c.start()
    l_cot, l_vision, l_proj, l_value, l_text = loads[3], loads[4], loads[5:-2], loads[-2], loads[-1]
    barrier = pltpu.get_barrier_semaphore()
    for p in peers:
        pl.semaphore_signal(barrier, inc=1, device_id={"grp": p}, device_id_type=MESH)
    for c in loads[-2:]:
        c.start()
    for i in range(1, tps):
        pl.semaphore_signal(barrier, inc=1, device_id={"tp": lax.rem(tp + i, tps)}, device_id_type=MESH)
    for i in range(1, pps):
        pl.semaphore_signal(barrier, inc=1, device_id={"pp": lax.rem(pp + i, pps)}, device_id_type=MESH)

    for c in loads[:3]:
        c.wait()
    t_row = target_v[...]
    t_col = to_col(t_row)
    same = t_col == t_row
    k_col = jnp.sum(jnp.where(same & (iota((img, img), 1) < iota((img, img), 0)), 1, 0), axis=1, keepdims=True)
    k_row = jnp.sum(jnp.where(same & (iota((img, img), 0) < iota((img, img), 1)), 1, 0), axis=0, keepdims=True)
    counts = jnp.sum(flag(t_col == iota((img, 128), 1)), axis=0, keepdims=True)
    sp_row = place_v[...]
    sp_col = to_col(sp_row)
    loss_f = loss_v[...].astype(F32)
    at_slot = flag(sp_col == iota((slots, seq), 1))
    mask_slot = jnp.sum(at_slot * loss_f, axis=1, keepdims=True)
    eye = iota((slots, slots), 0) == iota((slots, slots), 1)
    mask_row = jnp.sum(jnp.where(eye, mask_slot, 0.0), axis=0, keepdims=True)
    mask_sum = jnp.sum(loss_f, axis=1, keepdims=True)
    r8 = iota((8, 128), 0)
    meta = jnp.where(r8 == 0, counts, jnp.where(r8 == 1, mask_row, jnp.where(r8 == 2, mask_sum, 0.0)))
    xmeta[...] = meta.astype(BF)

    d_i = iota((4 * slots, 1), 0)
    d_from = slots * ((d_i // 4) % 4) + 4 * (d_i // 16) + d_i % 4
    shuffle = flag(iota((4 * slots, 4 * slots), 1) == d_from).astype(BF)
    l_cot.wait()
    y = mm(at_slot.astype(BF), cot_v[...]).astype(BF)
    ystack = jnp.concatenate([y[:, 128 * j : 128 * (j + 1)] for j in range(4)], axis=0)
    xcot[...] = mm(shuffle, ystack).astype(BF).reshape(groups, 16, 128)

    l_vision.wait()
    for i in range(parts):
        l_proj[i].wait()
        part = mm(vision_v[:, i * kchunk : (i + 1) * kchunk], wp_v[i * kchunk : (i + 1) * kchunk, :])
        if i == 0:
            emb_acc[...] = part
        else:
            emb_acc[...] += part
    l_value.wait()
    emb = emb_acc[...].astype(BF)
    for t in range(tps):
        if t % 2 == 0:
            res = mm(emb, wv_v[:, 128 * t : 128 * t + 256])
        piece = res[:, 128 * (t % 2) : 128 * (t % 2) + 128]
        for s in range(2):
            ipf[t % 2, t // 2, s] = piece[s * (img // 2) : (s + 1) * (img // 2)]

    lead = lambda ref, s: ref.at[..., s, :, :] if len(ref.shape) == 4 else ref.at[s]
    span = (pl.ds(0, cut), pl.ds(cut, dvis - cut))
    lane_cut = lambda ref, s: ref.at[..., span[s]]
    whole = [[lambda ref, s=s: lead(ref, s)] for s in range(2)]
    mids = ((0, cut // 256 * 128, cut), (cut, cut + (dvis - cut) // 256 * 128, dvis))
    parts_g = [[lambda ref, lo=lo, up=up: ref.at[..., pl.ds(lo, up - lo)] for lo, up in zip(m[:-1], m[1:])] for m in mids]
    red_i = Reduce(env, lead, whole, ipf, ipb, ipr, isb, ir1, ifd, ifu, i_send, i_recv)
    red_t = Reduce(env, lead, whole, tpf, tpb, tpr, tsb, tr1, tfd, tfu, t_send, t_recv)
    red_g = Reduce(env, lane_cut, parts_g, gpf, gpb, gpr, gsb, gr1, gfd, gfu, g_send, g_recv)

    pl.semaphore_wait(barrier, (tps - 1) + (groups - 1) + (pps - 1))

    red_i.start_pair(0)
    red_i.start_pair(1)

    def spread(src, dst, k, whole):
        for p in peers:
            pltpu.make_async_remote_copy(
                src if whole else src.at[p], dst.at[grp], a_send.at[k], a_recv.at[k],
                device_id={"grp": p}, device_id_type=MESH,
            ).start()

    spread(xcot, rcot, 0, False)

    l_text.wait()
    rows_out = seq // tps
    hr = rows_out // 2

    def text_part(n):
        cols = pl.ds(n * 256, 256)
        res = mm(text_v[...], wv_v[:, cols])
        for t in range(tps):
            for s in range(2):
                r0 = t * rows_out + s * hr
                tpf[t % 2, t // 2, s, :, cols] = res[r0 : r0 + hr]

    text_part(0)
    text_part(1)

    red_i.first(0)
    red_i.first(1)
    red_i.direct(0)
    red_i.direct(1)
    for n in range(2, kvd // 256):
        text_part(n)
    red_t.start_pair(0)
    red_t.start_pair(1)
    red_t.first(0)
    red_t.first(1)
    red_i.relay(0)
    red_i.relay(1)
    red_t.direct(0)
    red_t.direct(1)

    lane = iota((img, 4 * slots), 1)
    pick = jnp.concatenate(
        [flag(lane == 16 * t_col + 4 * j + k_col).astype(BF) for j in range(4)], axis=0
    )
    collected(rcot, a_recv.at[0], groups - 1)
    rcot[pl.ds(grp, 1)] = xcot[pl.ds(grp, 1)]
    got = mm(pick, rcot[...].reshape(4 * slots, 128)).astype(BF)
    mine = jnp.concatenate([got[img * j : img * (j + 1)] for j in range(4)], axis=1)
    chalf[pl.ds(core, 1)] = mine[None]
    swap = pltpu.make_async_remote_copy(
        chalf.at[core], chalf.at[core], s_sem.at[0], s_sem.at[1], device_id={"tp": env["partner"]}, device_id_type=MESH
    )
    swap.start()

    spread(xmeta, rmeta, 1, True)

    half_cols = lambda c: pl.ds(pl.multiple_of(c * half_kv, 128), half_kv)
    for n in range(0, width, 256):
        emb_acc[:, n : n + 256] = mm_nt(mine, wv_v[n : n + 256, half_cols(core)])
    swap.wait_recv()
    red_t.relay(0)
    red_t.relay(1)
    other = chalf[1 - core]
    for n in range(0, width, 256):
        emb_acc[:, n : n + 256] += mm_nt(other, wv_v[n : n + 256, half_cols(1 - core)])
    d_img = emb_acc[...].astype(BF)

    def grad_part(lo, up):
        res = mm_nt(d_img, wp_v[lo:up, :])
        for t in range(tps):
            gpf[t % 2, t // 2, :, lo:up] = res[8 * t : 8 * t + 8]

    first = cut // 256 * 128
    grad_part(0, first)

    r_slot = flag(iota((8 * groups, img), 0) == 8 * t_row + k_row).astype(BF)
    vals = red_i.end().reshape(img, 128).astype(BF)
    ximg[...] = mm(r_slot, vals).reshape(groups, 8, 128).astype(BF)
    spread(ximg, rimg, 2, False)
    grad_part(first, cut)
    red_g.start_pair(0)

    mid = cut + (dvis - cut) // 256 * 128
    grad_part(cut, mid)
    grad_part(mid, dvis)
    red_g.start_pair(1)
    red_g.first(0)

    red_g.first(1)
    red_g.direct(1)

    collected(rmeta, a_recv.at[1], groups - 1)
    rmeta[pl.ds(grp, 1)] = xmeta[...][None]
    metas = rmeta[...].astype(F32).reshape(8 * groups, 128).astype(BF)
    e_i, e_l = iota((groups, 8 * groups), 0), iota((groups, 8 * groups), 1)
    c_mat = mm(flag(e_l == 8 * e_i).astype(BF), metas)
    m_mat = mm(flag(e_l == 8 * e_i + 1).astype(BF), metas)
    s_mat = mm(flag(e_l == 8 * e_i + 2).astype(BF), metas)
    fan = flag(iota((groups, slots), 1) // cap == iota((groups, slots), 0)).astype(BF)
    used = lax.dot_general(
        c_mat.astype(BF), fan, (((0,), (0,)), ((), ())), preferred_element_type=F32
    )[:groups]
    k_of = (iota((groups, slots), 1) % cap).astype(F32)
    lost = jnp.sum(jnp.where(k_of < used, m_mat, 0.0)).reshape(1, 1)
    total = jnp.sum(s_mat[:, 0:1]).reshape(1, 1) - lost
    tot_s[...] = jnp.broadcast_to(total, (8, 128))
    tot_copies = []
    for i in range(1, pps):
        tot_copies.append(
            pltpu.make_async_remote_copy(
                tot_s, tot_r.at[i - 1], p_send.at[0], p_recv.at[0],
                device_id={"pp": lax.rem(pp + i, pps)}, device_id_type=MESH,
            )
        )
    for c in tot_copies:
        c.start()

    x_l, x_i = iota((slots, 8 * groups), 1), iota((slots, 8 * groups), 0)
    holds = (x_i == cap * (x_l // 8) + x_l % 8) & (x_l % 8 < cap)
    sp8 = jnp.sum(jnp.where(holds, sp_col + 1, 0), axis=0, keepdims=True) - 1
    c_me = jnp.sum(jnp.where(iota((groups, 128), 1) == grp, c_mat, 0.0), axis=1, keepdims=True)
    c8 = jnp.sum(jnp.where(e_l // 8 == e_i, c_me, 0.0), axis=0, keepdims=True)
    valid = (iota((1, 8 * groups), 1) % 8).astype(F32) < c8
    pos8 = jnp.where(valid, sp8, -1)
    put = flag(iota((seq, 8 * groups), 0) == pos8).astype(BF)
    collected(rimg, a_recv.at[2], groups - 1)
    rimg[pl.ds(grp, 1)] = ximg[pl.ds(grp, 1)]
    zs[...] = mm(put, rimg[...].astype(F32).reshape(8 * groups, 128).astype(BF)).astype(BF).reshape(tps, rows_out, 128)
    z_copies = []
    for i in (4, 3, 5, 2, 6, 1, 7):
        peer = lax.rem(tp + i, tps)
        z_copies.append(
            pltpu.make_async_remote_copy(
                zs.at[peer], zr.at[tp], z_send.at[0], z_recv.at[0], device_id={"tp": peer}, device_id_type=MESH
            )
        )
        z_copies[-1].start()

    red_g.direct(0)
    red_g.relay(0)
    red_g.relay(1)
    text_vals = red_t.end().reshape(rows_out, kvd)
    is_img = jnp.sum(flag(iota((rows_out, 8 * groups), 0) + rows_out * tp == pos8), axis=1, keepdims=True)
    collected(zr, z_recv.at[0], tps - 1)
    zr[pl.ds(tp, 1)] = zs[pl.ds(tp, 1)]
    for t in range(tps):
        cols = slice(128 * t, 128 * t + 128)
        values_out[:, cols] = jnp.where(is_img > 0.5, zr[t].astype(F32), text_vals[:, cols]).astype(BF)

    collected(tot_r, p_recv.at[0], pps - 1)
    text_total = tot_s[...]
    for i in range(1, pps):
        text_total = text_total + tot_r[i - 1]
    scale = (jnp.full((8, 128), float(pps * groups * seq), F32) / text_total)[:, 0:1]
    grad_out[...] = (red_g.end() * scale).astype(BF)

    for r in (red_i, red_t, red_g):
        r.drain()
    collected(xcot, a_send.at[0], groups - 1)
    collected(rmeta, a_send.at[1], groups - 1)
    collected(ximg, a_send.at[2], groups - 1)
    swap.wait_send()
    collected(zs, z_send.at[0], tps - 1)
    collected(tot_r, p_send.at[0], pps - 1)


def put_out(values, grads, values_out, grads_out, sems):
    copies = [
        pltpu.make_async_copy(values, values_out.at[0], sems.at[0]),
        pltpu.make_async_copy(grads, grads_out.at[0], sems.at[1]),
    ]
    for c in copies:
        c.start()
    for c in copies:
        c.wait()


def body(vision, text_embed, target, slot_place, loss_mask, w_proj, w_value, cotangent):
    groups, tps, pps = lax.axis_size("grp"), lax.axis_size("tp"), lax.axis_size("pp")
    img, dvis, width = vision.shape[1], vision.shape[2], w_proj.shape[1]
    seq, kvd, slots = text_embed.shape[1], w_value.shape[1], slot_place.shape[2]
    chips, parts = tps // 2, 5
    cut = dvis * 3 // 5 // 128 * 128
    rows, grows = seq // tps, img // tps
    vm = pltpu.VMEM
    dma = lambda *s: pltpu.SemaphoreType.DMA(s)

    def reduce_bufs(chunk):
        return [
            vm((2, chips) + chunk, F32), vm((chips,) + chunk, BF), vm((chips,) + chunk, BF), vm((chips,) + chunk, BF),
            vm(chunk, BF), vm(chunk, BF), vm(chunk, BF),
        ]

    scratch = (
        [vm((1, img), I32), vm((1, slots), I32), vm((1, seq), I32), vm((img, dvis), BF), vm((dvis, width), BF),
         vm((width, kvd), BF), vm((seq, width), BF), vm((seq, kvd // 2), BF), vm((img, width), F32)]
        + reduce_bufs((2, rows // 2, kvd))
        + reduce_bufs((2, img // 2, 128))
        + reduce_bufs((grows, dvis))
        + [vm((groups, 16, 128), BF), vm((groups, 16, 128), BF), vm((8, 128), BF), vm((groups, 8, 128), BF),
           vm((groups, 8, 128), BF), vm((groups, 8, 128), BF), vm((2, img, kvd // 2), BF),
           vm((tps, rows, 128), BF), vm((tps, rows, 128), BF), vm((8, 128), F32), vm((pps - 1, 8, 128), F32)]
        + [dma(7 + parts), dma(2), dma(5), dma(2), dma(5), dma(2), dma(7), dma(3), dma(3),
           dma(1), dma(1), dma(2), dma(1), dma(1)]
    )
    in_hbm = lambda a: pltpu.with_memory_space_constraint(a, pltpu.HBM)
    values, grads = pl.pallas_call(
        functools.partial(kernel, (groups, tps, pps, parts, cut)),
        out_shape=(
            jax.ShapeDtypeStruct((rows, kvd), BF),
            jax.ShapeDtypeStruct((grows, dvis), BF),
        ),
        in_specs=[pl.BlockSpec(memory_space=pl.ANY)] * 8,
        out_specs=(pl.BlockSpec(memory_space=pltpu.VMEM), pl.BlockSpec(memory_space=pltpu.VMEM)),
        scratch_shapes=scratch,
        compiler_params=pltpu.CompilerParams(
            collective_id=0, has_side_effects=True, vmem_limit_bytes=48 * 1024 * 1024
        ),
    )(
        *map(
            in_hbm,
            (target.reshape(1, img), slot_place.reshape(1, slots), loss_mask, vision, w_proj, w_value, text_embed, cotangent),
        )
    )
    return pl.pallas_call(
        put_out,
        out_shape=(jax.ShapeDtypeStruct((1, rows, kvd), BF), jax.ShapeDtypeStruct((1, grows, dvis), BF)),
        in_specs=[pl.BlockSpec(memory_space=pltpu.VMEM)] * 2,
        out_specs=(pl.BlockSpec(memory_space=pltpu.HBM), pl.BlockSpec(memory_space=pltpu.HBM)),
        scratch_shapes=[dma(2)],
        compiler_params=pltpu.CompilerParams(vmem_limit_bytes=4 * 1024 * 1024),
    )(values, grads)


def solution(mesh):
    in_specs = (
        P("pp", "grp", None),
        P("pp", "grp", "tp"),
        P("pp", "grp", None),
        P("pp", "grp", None),
        P("pp", "grp"),
        P(None, "tp"),
        P("tp", None),
        P("pp", "grp", None),
    )
    out_specs = (P("pp", ("grp", "tp"), None), P("pp", ("grp", "tp"), None))
    return jax.shard_map(body, mesh=mesh, in_specs=in_specs, out_specs=out_specs, check_vma=False)
```
